512 devices in a mesh: wall: 8 (over x, z_hi), row: 64 (over z_lo, y, core).
Axes of the slice: x: 4, y: 8, z: 8 (z_hi: 2, z_lo: 4; z = z_hi * 4 + z_lo), core: 2. Of those that a mesh axis runs over, the one named last changes fastest.
Arguments:
- thermal_scalars: float32 [2, 32, 1024, 1024], P(None, 'wall', 'row'), may hold values from -6 to 6
- conductive_number: float32 [2, 32], P(None, 'wall'), may hold values from 0.05 to 0.45
Outputs:
- advanced: float32 [2, 32, 1024, 1024], P(None, 'wall', 'row')
The draws below stay inside these ranges and needn't reach their ends.
All inputs are finite; a program needn't handle non-finite values.
Results may differ from the reference program's by a relative error of at most 0.00007.
Values sent between devices are 32-bit elements; how exact they have to be, the bound alone decides.
A program may use at most 64 MiB of HBM per device.

```python
import math
import jax
import jax.numpy as jnp

DOWNSTREAM_COUNT = 1024
LATERAL_COUNT = 1024
STEPS = 3
NORMAL_LAYERS = 32


def levels(stream_key, shape, split, smallest, high):
    def one(dim, blocks):
        heights = jax.random.uniform(jax.random.fold_in(jax.random.fold_in(stream_key, 6), dim), (blocks,), jnp.float32, smallest / len(split), high / len(split))
        return jnp.repeat(jnp.exp(heights), shape[dim] // blocks).reshape((-1,) + (1,) * (len(shape) - dim - 1))

    gain = one(*split[0])
    for cut in split[1:]:
        gain = gain * one(*cut)
    return gain


def normal_values(key, shape, width, most, shards=(), kind=jnp.bfloat16):
    loudness = levels(key, shape, shards, -0.22, 0.18) if shards else 1.0
    result = jax.random.normal(key, shape, jnp.float32) * width * loudness
    return jnp.minimum(jnp.maximum(result, -most), most).astype(kind)


def setup_inputs(seed: int = 0) -> dict:
    streams_of = jax.random.split(jax.random.key(seed), 3)
    return {
        "thermal_scalars": normal_values(streams_of[0], (2, NORMAL_LAYERS, DOWNSTREAM_COUNT, LATERAL_COUNT), 1.0, 6.0, ((1, 8), (2, 64)), jnp.float32),
        "conductive_number": jnp.clip(jnp.exp(math.log(0.45) - 2.1972245 * jax.random.uniform(streams_of[1], (2, NORMAL_LAYERS), jnp.float32) ** levels(streams_of[1], (2, NORMAL_LAYERS), ((1, 8),), -0.2, 0.2)), 0.05, 0.45),
    }


def signed_square(waves, length):
    signed = jnp.where(waves > length // 2, waves - length, waves).astype(jnp.int32)
    scaled = (2.0 * math.pi / length) * signed.astype(jnp.float32)
    return scaled * scaled


def reference(thermal_scalars, conductive_number):
    complex_combined_fields = jnp.fft.fft2(thermal_scalars[0] + 1j * thermal_scalars[1], axes=(1, 2))
    mirror = jnp.roll(jnp.flip(complex_combined_fields, axis=(1, 2)), 1, axis=(1, 2))
    first_hat = 0.5 * (complex_combined_fields + jnp.conj(mirror))
    second_hat = -0.5j * (complex_combined_fields - jnp.conj(mirror))
    square_x = signed_square(jnp.arange(DOWNSTREAM_COUNT, dtype=jnp.int32), DOWNSTREAM_COUNT)
    square_y = signed_square(jnp.arange(LATERAL_COUNT, dtype=jnp.int32), LATERAL_COUNT)
    wave_sq = square_x[:, None] + square_y[None, :]
    results = []
    for scalar, scalar_field in enumerate([first_hat, second_hat]):
        rate_col = conductive_number[scalar][:, None, None]
        damping = jnp.exp(-rate_col * wave_sq[None, :, :])
        for substep in range(STEPS):
            padded = jnp.pad(scalar_field, ((1, 1), (0, 0), (0, 0)))
            curve_term = padded[2:] + padded[:-2] - 2.0 * scalar_field
            scalar_field = damping * (scalar_field + rate_col * curve_term)
        results.append(scalar_field)
    joined = results[0] + 1j * results[1]
    spatial = jnp.fft.ifft2(joined, axes=(1, 2))
    return jnp.stack([jnp.real(spatial), jnp.imag(spatial)]).astype(jnp.float32)
```

```python
import functools
import math

import jax
import jax.numpy as jnp
import numpy as np
from jax import lax
from jax.experimental import pallas as pl
from jax.experimental.pallas import tpu as pltpu
from jax.sharding import PartitionSpec as P

STEPS = 3
MESH = pl.DeviceIdType.MESH
N = 1024
COLUMN = 16
PLANE = 32
WALLS = 8
SPECIAL = 384
HALF = math.sqrt(0.5)


def halves(table):
    table = np.asarray(table, np.float32)
    high = table.astype(jnp.bfloat16)
    low = (table - high.astype(np.float32)).astype(jnp.bfloat16)
    return np.stack([high, low])


def y_tables():
    b = np.arange(128)[None, :]
    m = np.arange(128)[:, None]
    forward, inverse = [], []
    for n in (1, 2, 3):
        angle = 2 * np.pi * ((b * (8 * m + n)) % N) / N
        c, s = np.cos(angle), np.sin(angle)
        forward.append(np.concatenate([c, s], 1))
        inverse.append(np.block([[c, s], [-s, c]]))
    m = m[:64]
    zero = 2 * np.pi * ((b * 8 * m) % N) / N
    four = 2 * np.pi * ((b * (8 * m + 4)) % N) / N
    c0, s0, c4, s4 = np.cos(zero), np.sin(zero), np.cos(four), np.sin(four)
    flip = np.where(b % 2 == 0, 1.0, -1.0)
    s0[:1] = -flip
    forward.append(np.block([[c0, s0], [c4, s4]]))
    c0[:1] *= 0.5
    s0[:1] *= 0.5
    none = np.zeros_like(c0)
    inverse.append(np.block([[c0, none], [none, c4], [-s0, none], [none, -s4]]))
    return halves(np.stack(forward)), halves(np.stack(inverse))


def x_tables():
    n = np.arange(64)
    angle = 2 * np.pi * ((n[:, None] * n[None, :]) % 64) / 64
    c, s = np.cos(angle), np.sin(angle)
    first = np.concatenate([c, s], 0)
    last = np.concatenate([c, s], 1)
    i = np.arange(16)
    small = 2 * np.pi * ((i[:, None] * i[None, :]) % 16) / 16
    c, s = np.cos(small), np.sin(small)
    into = np.zeros((2, 4, 16, 4, 2, 16))
    back = np.zeros((4, 2, 16, 2, 4, 16))
    for z in range(4):
        into[0, z, :, z, 0] = c
        into[0, z, :, z, 1] = -s
        into[1, z, :, z, 0] = s
        into[1, z, :, z, 1] = c
        back[z, 0, :, 0, z] = c
        back[z, 0, :, 1, z] = s
        back[z, 1, :, 0, z] = -s
        back[z, 1, :, 1, z] = c
    turned = np.stack([-into[1], into[0]])
    into = np.concatenate([into.reshape(128, 128), turned.reshape(128, 128)], 0)
    back_turned = np.stack([-back[:, :, :, 1], back[:, :, :, 0]], 3)
    back = np.concatenate([back.reshape(128, 128), back_turned.reshape(128, 128)], 1)
    lane = np.arange(128)
    turn = 2 * np.pi * (n[:, None] * (lane % 16)[None, :]) / N
    wave = n[:, None] + 64 * (lane % 16)[None, :]
    wave = np.where(wave > N // 2, wave - N, wave)
    square = (2 * np.pi / N * wave) ** 2
    plain = np.stack([np.cos(turn), np.sin(turn), square]).astype(np.float32)
    return halves(first), halves(last), halves(into), halves(back), plain


def split(value):
    high = value.astype(jnp.bfloat16)
    return high, (value - high.astype(jnp.float32)).astype(jnp.bfloat16)


def product(left, right, dims):
    dot = functools.partial(
        lax.dot_general, dimension_numbers=(dims, ((), ())), preferred_element_type=jnp.float32
    )
    return dot(left[0], right[0]) + (dot(left[0], right[1]) + dot(left[1], right[0]))


def pair(ref, *index):
    return ref[(0, *index)], ref[(1, *index)]


def to_waves(field, table, out, s):
    f = [field[:, 128 * a : 128 * a + 128] for a in range(8)]
    s04, d04, s26, d26 = f[0] + f[4], f[0] - f[4], f[2] + f[6], f[2] - f[6]
    s15, d15, s37, d37 = f[1] + f[5], f[1] - f[5], f[3] + f[7], f[3] - f[7]
    even, odd = s04 + s26, s15 + s37
    less, more = HALF * (d15 - d37), HALF * (d15 + d37)
    none = jnp.zeros_like(even)
    parts = [
        (d04 + less, -d26 - more),
        (s04 - s26, s37 - s15),
        (d04 - less, d26 - more),
    ]
    for j, (re, im) in enumerate(parts):
        both = jnp.concatenate(
            [jnp.concatenate([re, im], 1), jnp.concatenate([im, -re], 1)], 0
        )
        waves = product(pair(table, j), split(both), ((1,), (1,)))
        out[s, 8 * j : 8 * j + 8] = waves.reshape(8, 16, 128)
    for j, re in enumerate((even + odd, even - odd)):
        both = jnp.concatenate(
            [jnp.concatenate([re, none], 1), jnp.concatenate([none, -re], 1)], 0
        )
        rows = slice(64 * j, 64 * j + 64)
        waves = product(pair(table, 3, rows), split(both), ((1,), (1,)))
        out[s, 24 + 4 * j : 28 + 4 * j] = waves.reshape(4, 16, 128)


def from_waves(waves, table, out, s):
    u = []
    for j in range(4):
        lines = waves[s, 8 * j : 8 * j + 8].reshape(128, 128).T
        both = jnp.concatenate([lines[:64], lines[64:]], 1)
        u.append(product(split(both), pair(table, j), ((1,), (0,))))
    (re1, im1), (re2, im2), (re3, im3), (z0, z4) = [(v[:, :128], v[:, 128:]) for v in u]
    plus, minus = z0 + z4, z0 - z4
    even = [plus + re2, minus - im2, plus - re2, minus + im2]
    odd = [
        re1 + re3,
        HALF * ((re1 - im1) - (re3 + im3)),
        im3 - im1,
        HALF * ((re3 - im3) - (re1 + im1)),
    ]
    for a in range(4):
        out[s, :, :, 128 * a : 128 * a + 128] = (even[a] + odd[a]).reshape(4, 16, 128)
        out[s, :, :, 128 * a + 512 : 128 * a + 640] = (even[a] - odd[a]).reshape(4, 16, 128)


def to_spectrum(lines, first, into, plain, out, s):
    cos, sin = plain[0], plain[1]
    for w in range(WALLS):
        block = lines[s, 4 * w : 4 * w + 4].reshape(64, 128)
        both = product(pair(first), split(block), ((1,), (0,)))
        c, t = both[:64], both[64:]
        turned = jnp.concatenate([c * cos - t * sin, c * sin + t * cos], 1)
        out[s, w] = product(split(turned), pair(into), ((1,), (0,)))


def set_damping(rates, plain, square, out, s):
    q = plain[2] + square
    for w in range(WALLS):
        rate = jnp.concatenate([rates[w, s]] * 8, 0)
        out[s, w] = jnp.exp(-rate * q)


def diffuse(spectrum, rates, damping, out, s):
    lane = lax.broadcasted_iota(jnp.int32, (8, 128), 1)
    low, high = lane < 32, lane >= 96
    none = jnp.zeros((8, 128), jnp.float32)
    for block in range(8):
        rows = slice(8 * block, 8 * block + 8)
        f = [spectrum[s, w, rows] for w in range(WALLS)]
        for step in range(STEPS):
            new = []
            for w in range(WALLS):
                above = f[w + 1] if w + 1 < WALLS else none
                below = f[w - 1] if w else none
                up = pltpu.roll(jnp.where(low, above, f[w]), 96, 1)
                down = pltpu.roll(jnp.where(high, below, f[w]), 32, 1)
                curve = up + down - 2.0 * f[w]
                new.append(damping[s, w, rows] * (f[w] + rates[w, s] * curve))
            f = new
        for w in range(WALLS):
            out[w, rows] = f[w]


def from_spectrum(spectrum, back, last, plain, w):
    cos, sin = plain[0], plain[1]
    both = product(split(spectrum[w]), pair(back), ((1,), (0,)))
    value, turned = both[:, :128], both[:, 128:]
    stacked = jnp.concatenate([value * cos + turned * sin, turned * cos - value * sin], 0)
    return product(pair(last), split(stacked), ((1,), (0,)))


def kernel(
    x_ref, rate_ref, yf, yi, first, last, into, back, plain, out_ref,
    sent, middle, lines, spectrum, damped, damping, rates,
    returned, middle_back, waves, send_sem, recv_sem, rate_sem,
):
    wall, row = lax.axis_index("wall"), lax.axis_index("row")
    low, column = row // COLUMN, row % COLUMN
    plane = wall * 4 + low
    device = wall * 64 + row

    def column_peer(i):
        y, core = column // 2, column % 2
        return lax.rem(y + i // 2, 8) * 2 + lax.rem(core + i, 2)

    def plane_peer(i):
        x, z = plane // 8, plane % 8
        return lax.rem(x + i // 8, 4) * 8 + lax.rem(z + i, 8)

    def column_id(c):
        return wall, low * COLUMN + c

    def plane_id(p):
        return p // 4, lax.rem(p, 4) * COLUMN + column

    barrier = pltpu.get_barrier_semaphore()

    @pl.loop(1, PLANE)
    def _(i):
        pl.semaphore_signal(barrier, inc=1, device_id=plane_id(plane_peer(i)), device_id_type=MESH)

    @pl.loop(1, COLUMN)
    def _(i):
        pl.semaphore_signal(barrier, inc=1, device_id=column_id(column_peer(i)), device_id_type=MESH)

    def over_column(src, dst, k):
        pltpu.make_async_copy(src.at[:, column], dst.at[:, column], recv_sem.at[k]).start()

        @pl.loop(1, COLUMN)
        def _(i):
            c = column_peer(COLUMN - i)
            pltpu.make_async_remote_copy(
                src_ref=src.at[:, c], dst_ref=dst.at[:, column],
                send_sem=send_sem.at[k], recv_sem=recv_sem.at[k],
                device_id=column_id(c), device_id_type=MESH,
            ).start()

        def sent_all():
            part = pl.ds(0, COLUMN - 1)
            pltpu.make_async_copy(src.at[:, part], dst.at[:, part], send_sem.at[k]).wait()

        return lambda: pltpu.make_async_copy(src, dst, recv_sem.at[k]).wait(), sent_all

    def over_plane(src, dst, k):
        pltpu.make_async_copy(src.at[plane], dst.at[plane], recv_sem.at[k]).start()

        @pl.loop(1, PLANE)
        def _(i):
            p = plane_peer(PLANE - i)
            pltpu.make_async_remote_copy(
                src_ref=src.at[p], dst_ref=dst.at[plane],
                send_sem=send_sem.at[k], recv_sem=recv_sem.at[k],
                device_id=plane_id(p), device_id_type=MESH,
            ).start()

        def sent_all():
            part = pl.ds(0, PLANE - 1)
            pltpu.make_async_copy(src.at[part], dst.at[part], send_sem.at[k]).wait()

        return lambda: pltpu.make_async_copy(src, dst, recv_sem.at[k]).wait(), sent_all

    zone = lax.broadcasted_iota(jnp.int32, (8, 128), 1) // 32
    for s in range(2):
        value = jnp.full((8, 128), rate_ref[s, 0], jnp.float32)
        for z in range(1, 4):
            value = jnp.where(zone == z, rate_ref[s, z], value)
        rates[wall, s] = value
    to_waves(x_ref[0].reshape(64, N), yf, sent, 0)
    pl.semaphore_wait(barrier, PLANE + COLUMN - 2)
    a1, a1_sent = over_column(sent.at[0], middle.at[0], 0)
    to_waves(x_ref[1].reshape(64, N), yf, sent, 1)
    b1, b1_sent = over_plane(sent.at[1], middle.at[1], 1)

    @pl.loop(1, WALLS)
    def _(i):
        pltpu.make_async_remote_copy(
            src_ref=rates.at[wall], dst_ref=rates.at[wall],
            send_sem=rate_sem.at[0], recv_sem=rate_sem.at[1],
            device_id=(lax.rem(wall + i, WALLS), row), device_id_type=MESH,
        ).start()

    a1()
    a2, a2_sent = over_plane(middle.at[0], lines.at[0], 2)
    b1()
    b2, b2_sent = over_column(middle.at[1], lines.at[1], 3)

    group = pl.ds(0, WALLS - 1)
    pltpu.make_async_copy(rates.at[group], rates.at[group], rate_sem.at[1]).wait()
    group_of, m = device // 128, device % 128
    wave = jnp.where(group_of < 3, 8 * m + group_of + 1, 8 * lax.rem(m, 64) + 4 * (m // 64))
    wave = jnp.where(wave > N // 2, wave - N, wave)
    scale = 2.0 * math.pi / N
    scaled = scale * wave.astype(jnp.float32)
    square = scaled * scaled
    for s in range(2):
        set_damping(rates, plain, square, damping, s)

    passes = jnp.where(device == SPECIAL, 2, 1)
    part = lax.broadcasted_iota(jnp.int32, (64, 128), 1)

    def through(s):
        to_spectrum(lines, first, into, plain, spectrum, s)

        @pl.loop(0, passes)
        def _(p):
            @pl.when(p == 1)
            def _():
                set_damping(rates, plain, (scale * (N // 2)) ** 2, damping, s)

            diffuse(spectrum, rates, damping, damped, s)
            for w in range(WALLS):
                result = from_spectrum(damped, back, last, plain, w)
                at = slice(4 * w, 4 * w + 4)

                @pl.when(p == 0)
                def _():
                    returned[s, at] = result.reshape(4, 16, 128)

                @pl.when(p == 1)
                def _():
                    kept = returned[s, at].reshape(64, 128)
                    returned[s, at] = jnp.where(part < 64, kept, result).reshape(4, 16, 128)

    a2()
    through(0)
    a3, a3_sent = over_column(returned.at[0], middle_back.at[0], 4)
    b2()
    through(1)
    b3, b3_sent = over_plane(returned.at[1], middle_back.at[1], 5)
    a3()
    a4, a4_sent = over_plane(middle_back.at[0], waves.at[0], 6)
    b3()
    b4, b4_sent = over_column(middle_back.at[1], waves.at[1], 7)
    a4()
    from_waves(waves, yi, out_ref, 0)
    b4()
    from_waves(waves, yi, out_ref, 1)
    pltpu.make_async_copy(rates.at[group], rates.at[group], rate_sem.at[0]).wait()
    for done in (a1_sent, b1_sent, a2_sent, b2_sent, a3_sent, b3_sent, a4_sent, b4_sent):
        done()


def per_device(thermal_scalars, conductive_number):
    tables = [*y_tables(), *x_tables()]
    yf, yi, first, last, into, back, plain = map(jnp.asarray, tables)
    block = pltpu.VMEM((2, PLANE, COLUMN, 128), jnp.float32)
    cube = pltpu.VMEM((2, WALLS, 64, 128), jnp.float32)
    vmem = pl.BlockSpec(memory_space=pltpu.VMEM)
    result = pl.pallas_call(
        kernel,
        out_shape=jax.ShapeDtypeStruct(thermal_scalars.shape, jnp.float32),
        in_specs=[vmem, pl.BlockSpec(memory_space=pltpu.SMEM)] + [vmem] * 7,
        out_specs=vmem,
        scratch_shapes=[
            block, block, block, cube, pltpu.VMEM((WALLS, 64, 128), jnp.float32), cube,
            pltpu.VMEM((WALLS, 2, 8, 128), jnp.float32),
            block, block, block,
            pltpu.SemaphoreType.DMA((8,)), pltpu.SemaphoreType.DMA((8,)),
            pltpu.SemaphoreType.DMA((2,)),
        ],
        compiler_params=pltpu.CompilerParams(collective_id=0, has_side_effects=True),
    )(thermal_scalars, conductive_number, yf, yi, first, last, into, back, plain)
    return result * (2.0 / (N * N))


def solution(mesh):
    return jax.shard_map(
        per_device,
        mesh=mesh,
        in_specs=(P(None, "wall", "row", None), P(None, "wall")),
        out_specs=P(None, "wall", "row", None),
        check_vma=False,
    )
```

```python
import functools
import math

import jax
import jax.numpy as jnp
import numpy as np
from jax import lax
from jax.experimental import pallas as pl
from jax.experimental.pallas import tpu as pltpu
from jax.sharding import PartitionSpec as P

STEPS = 3
MESH = pl.DeviceIdType.MESH
N = 1024
COLUMN = 16
PLANE = 32
WALLS = 8
SPECIAL = 384
HALF = math.sqrt(0.5)
VMEM_LIMIT = 62 << 20


def halves(table):
    table = np.asarray(table, np.float32)
    high = table.astype(jnp.bfloat16)
    low = (table - high.astype(np.float32)).astype(jnp.bfloat16)
    return np.stack([high, low])


def y_tables():
    b = np.arange(128)[None, :]
    m = np.arange(128)[:, None]
    forward, inverse = [], []
    for n in (1, 2, 3):
        angle = 2 * np.pi * ((b * (8 * m + n)) % N) / N
        c, s = np.cos(angle), np.sin(angle)
        forward.append(np.concatenate([c, s], 1))
        inverse.append(np.block([[c, s], [-s, c]]))
    m = m[:64]
    zero = 2 * np.pi * ((b * 8 * m) % N) / N
    four = 2 * np.pi * ((b * (8 * m + 4)) % N) / N
    c0, s0, c4, s4 = np.cos(zero), np.sin(zero), np.cos(four), np.sin(four)
    flip = np.where(b % 2 == 0, 1.0, -1.0)
    s0[:1] = -flip
    forward.append(np.block([[c0, s0], [c4, s4]]))
    c0[:1] *= 0.5
    s0[:1] *= 0.5
    none = np.zeros_like(c0)
    inverse.append(np.block([[c0, none], [none, c4], [-s0, none], [none, -s4]]))
    return halves(np.stack(forward)), halves(np.stack(inverse))


def x_tables():
    n = np.arange(64)
    angle = 2 * np.pi * ((n[:, None] * n[None, :]) % 64) / 64
    c, s = np.cos(angle), np.sin(angle)
    first = np.concatenate([c, s], 0)
    last = np.concatenate([c, s], 1)
    i = np.arange(16)
    small = 2 * np.pi * ((i[:, None] * i[None, :]) % 16) / 16
    c, s = np.cos(small), np.sin(small)
    into = np.zeros((2, 2, 4, 16, 4, 2, 16))
    back = np.zeros((4, 2, 16, 2, 2, 4, 16))
    for part in range(2):
        for z in range(4):
            into[0, part, z, :, z, part] = c + s
            into[1, part, z, :, z, part] = c - s
            back[z, part, :, 0, part, z] = c + s
            back[z, part, :, 1, part, z] = c - s
    into, back = into.reshape(256, 128), back.reshape(128, 256)
    lane = np.arange(128)
    turn = 2 * np.pi * (n[:, None] * (lane % 16)[None, :]) / N
    wave = n[:, None] + 64 * (lane % 16)[None, :]
    wave = np.where(wave > N // 2, wave - N, wave)
    square = (2 * np.pi / N * wave) ** 2
    plain = np.stack([np.cos(turn), np.sin(turn), square]).astype(np.float32)
    return halves(first), halves(last), halves(into), halves(back), plain


def split(value):
    high = value.astype(jnp.bfloat16)
    return high, (value - high.astype(jnp.float32)).astype(jnp.bfloat16)


def product(left, right, dims):
    dot = functools.partial(
        lax.dot_general, dimension_numbers=(dims, ((), ())), preferred_element_type=jnp.float32
    )
    return dot(left[0], right[0]) + (dot(left[0], right[1]) + dot(left[1], right[0]))


def pair(ref, *index):
    return ref[(0, *index)], ref[(1, *index)]


def to_waves(field, table, out, s):
    f = [field[:, 128 * a : 128 * a + 128] for a in range(8)]
    s04, d04, s26, d26 = f[0] + f[4], f[0] - f[4], f[2] + f[6], f[2] - f[6]
    s15, d15, s37, d37 = f[1] + f[5], f[1] - f[5], f[3] + f[7], f[3] - f[7]
    even, odd = s04 + s26, s15 + s37
    less, more = HALF * (d15 - d37), HALF * (d15 + d37)
    none = jnp.zeros_like(even)
    parts = [
        (d04 + less, -d26 - more),
        (s04 - s26, s37 - s15),
        (d04 - less, d26 - more),
    ]
    for j, (re, im) in enumerate(parts):
        both = jnp.concatenate(
            [jnp.concatenate([re, im], 1), jnp.concatenate([im, -re], 1)], 0
        )
        waves = product(pair(table, j), split(both), ((1,), (1,)))
        out[s, 8 * j : 8 * j + 8] = waves.reshape(8, 16, 128)
    for j, re in enumerate((even + odd, even - odd)):
        both = jnp.concatenate(
            [jnp.concatenate([re, none], 1), jnp.concatenate([none, -re], 1)], 0
        )
        rows = slice(64 * j, 64 * j + 64)
        waves = product(pair(table, 3, rows), split(both), ((1,), (1,)))
        out[s, 24 + 4 * j : 28 + 4 * j] = waves.reshape(4, 16, 128)


def from_waves(waves, table, out, s):
    u = []
    for j in range(4):
        lines = waves[s, 8 * j : 8 * j + 8].reshape(128, 128).T
        both = jnp.concatenate([lines[:64], lines[64:]], 1)
        u.append(product(split(both), pair(table, j), ((1,), (0,))))
    (re1, im1), (re2, im2), (re3, im3), (z0, z4) = [(v[:, :128], v[:, 128:]) for v in u]
    plus, minus = z0 + z4, z0 - z4
    even = [plus + re2, minus - im2, plus - re2, minus + im2]
    odd = [
        re1 + re3,
        HALF * ((re1 - im1) - (re3 + im3)),
        im3 - im1,
        HALF * ((re3 - im3) - (re1 + im1)),
    ]
    for a in range(4):
        out[s, :, :, 128 * a : 128 * a + 128] = (even[a] + odd[a]).reshape(4, 16, 128)
        out[s, :, :, 128 * a + 512 : 128 * a + 640] = (even[a] - odd[a]).reshape(4, 16, 128)


def to_spectrum(lines, first, into, plain, out, s, w):
    cos, sin = plain[0], plain[1]
    block = lines[s, pl.ds(4 * w, 4)].reshape(64, 128)
    both = product(pair(first), split(block), ((1,), (0,)))
    c, t = both[:64], both[64:]
    turned = jnp.concatenate([c * cos - t * sin, c * sin + t * cos], 1)
    out[s, w] = product(split(turned), pair(into), ((1,), (0,)))


def set_damping(rates, plain, square, out, s):
    q = plain[2] + square
    for w in range(WALLS):
        rate = jnp.concatenate([rates[w, s]] * 8, 0)
        out[s, w] = jnp.exp(-rate * q)


def diffuse(spectrum, rates, damping, out, s):
    lane = lax.broadcasted_iota(jnp.int32, (8, 128), 1)
    low, high = lane < 32, lane >= 96
    none = jnp.zeros((8, 128), jnp.float32)
    for block in range(8):
        rows = slice(8 * block, 8 * block + 8)
        f = [spectrum[s, w, rows] for w in range(WALLS)]
        for step in range(STEPS):
            new = []
            for w in range(WALLS):
                above = f[w + 1] if w + 1 < WALLS else none
                below = f[w - 1] if w else none
                up = pltpu.roll(jnp.where(low, above, f[w]), 96, 1)
                down = pltpu.roll(jnp.where(high, below, f[w]), 32, 1)
                curve = up + down - 2.0 * f[w]
                new.append(damping[s, w, rows] * (f[w] + rates[w, s] * curve))
            f = new
        for w in range(WALLS):
            out[w, rows] = f[w]


def from_spectrum(spectrum, back, last, plain, w):
    cos, sin = plain[0], plain[1]
    both = product(split(spectrum[w]), pair(back), ((1,), (0,)))
    value, turned = both[:, :128], both[:, 128:]
    stacked = jnp.concatenate([value * cos + turned * sin, turned * cos - value * sin], 0)
    return product(pair(last), split(stacked), ((1,), (0,)))


def kernel(
    x_hbm, rate_ref, yf_hbm, yi_hbm, first_hbm, last_hbm, into_hbm, back_hbm, plain_hbm, out_ref,
    x_ref, yf, yi, first, last, into, back, plain,
    sent, middle, lines, spectrum, damped, damping, rates,
    returned, middle_back, waves, load_sem, send_sem, recv_sem, rate_sem,
):
    wall, row = lax.axis_index("wall"), lax.axis_index("row")
    low, column = row // COLUMN, row % COLUMN
    plane = wall * 4 + low
    device = wall * 64 + row
    x, z, y, core = plane // 8, plane % 8, column // 2, column % 2

    loads = [
        (x_hbm.at[0], x_ref.at[0]), (yf_hbm, yf), (x_hbm.at[1], x_ref.at[1]), (plain_hbm, plain),
        (first_hbm, first), (into_hbm, into), (back_hbm, back), (last_hbm, last), (yi_hbm, yi),
    ]
    loads = [pltpu.make_async_copy(*refs, load_sem.at[k]) for k, refs in enumerate(loads)]
    for load in loads[:3]:
        load.start()

    def column_id(c):
        return wall, low * COLUMN + c

    def plane_id(p):
        return p // 4, lax.rem(p, 4) * COLUMN + column

    def column_peer(h, i):
        half = (y // 4 + 1 - h) % 2
        return (half * 4 + (y + i // 2) % 4) * 2 + (core + i) % 2

    def plane_peer(h, i):
        half = (x // 2 + 1 - h) % 2
        return (half * 2 + (x + i // 8) % 2) * 8 + (z + i) % 8

    barrier = pltpu.get_barrier_semaphore()
    for h in range(2):

        @pl.loop(h, 16)
        def _(i):
            to = plane_id(plane_peer(h, i))
            pl.semaphore_signal(barrier, inc=1, device_id=to, device_id_type=MESH)

        @pl.loop(h, 8)
        def _(i):
            to = column_id(column_peer(h, i))
            pl.semaphore_signal(barrier, inc=1, device_id=to, device_id_type=MESH)

    for load in loads[3:]:
        load.start()

    whole_x, whole_y = pl.ds(0, PLANE), pl.ds(0, COLUMN)
    half_x = [pl.ds(pl.multiple_of((x // 2 + 1 - h) % 2 * 16, 16), 16) for h in range(2)]
    half_y = [pl.ds(pl.multiple_of((y // 4 + 1 - h) % 2 * 8, 8), 8) for h in range(2)]
    done = []

    def remote(src, dst, k, to):
        pltpu.make_async_remote_copy(
            src_ref=src, dst_ref=dst, send_sem=send_sem.at[k], recv_sem=recv_sem.at[k],
            device_id=to, device_id_type=MESH,
        ).start()

    def await_block(src, dst, sem, rows, columns):
        part = (pl.ds(0, rows), pl.ds(0, columns))
        return pltpu.make_async_copy(src.at[part], dst.at[part], sem).wait

    def over_column(src, dst, k, xs, n, halves):
        if 1 in halves:
            pltpu.make_async_copy(src.at[xs, column], dst.at[xs, column], recv_sem.at[k]).start()
        for h in halves:

            @pl.loop(h, 8)
            def _(i):
                c = column_peer(h, i)
                remote(src.at[xs, c], dst.at[xs, column], k, column_id(c))

        count = 8 * len(halves)
        done.append(await_block(src, dst, send_sem.at[k], n, count - (1 in halves)))
        return await_block(src, dst, recv_sem.at[k], n, count)

    def to_planes(src, dst, k, ys, h):
        if h:
            pltpu.make_async_copy(src.at[plane, ys], dst.at[plane, ys], recv_sem.at[k]).start()

        @pl.loop(h, 16)
        def _(i):
            p = plane_peer(h, i)
            remote(src.at[p, ys], dst.at[plane, ys], k, plane_id(p))

    def over_plane(src, dst, k, ys, n, halves):
        for h in halves:
            to_planes(src, dst, k, ys, h)
        count = 16 * len(halves)
        done.append(await_block(src, dst, send_sem.at[k], count - (1 in halves), n))
        return await_block(src, dst, recv_sem.at[k], count, n)

    zone = lax.broadcasted_iota(jnp.int32, (8, 128), 1) // 32
    for s in range(2):
        value = jnp.full((8, 128), rate_ref[s, 0], jnp.float32)
        for j in range(1, 4):
            value = jnp.where(zone == j, rate_ref[s, j], value)
        rates[wall, s] = value
    for s in range(2):
        if s == 0:
            loads[1].wait()
        loads[2 * s].wait()
        to_waves(x_ref[s].reshape(64, N), yf, sent, s)
    pl.semaphore_wait(barrier, PLANE + COLUMN - 2)

    both = (0, 1)
    a1, b1, a2, b2 = [], [], [], []
    for h in both:
        a1.append(over_column(sent.at[0], middle.at[0], h, half_x[h], 16, both))
        b1.append(over_plane(sent.at[1], middle.at[1], 2 + h, half_y[h], 8, both))

    @pl.loop(1, WALLS)
    def _(i):
        pltpu.make_async_remote_copy(
            src_ref=rates.at[wall], dst_ref=rates.at[wall],
            send_sem=rate_sem.at[0], recv_sem=rate_sem.at[1],
            device_id=(lax.rem(wall + i, WALLS), row), device_id_type=MESH,
        ).start()

    for h in both:
        a1[h]()
        a2.append(over_plane(middle.at[0], lines.at[0], 4 + h, whole_y, COLUMN, (h,)))
        b1[h]()
        b2.append(over_column(middle.at[1], lines.at[1], 6 + h, whole_x, PLANE, (h,)))

    group = pl.ds(0, WALLS - 1)
    pltpu.make_async_copy(rates.at[group], rates.at[group], rate_sem.at[1]).wait()
    for load in loads[3:]:
        load.wait()
    group_of, m = device // 128, device % 128
    wave = jnp.where(group_of < 3, 8 * m + group_of + 1, 8 * lax.rem(m, 64) + 4 * (m // 64))
    wave = jnp.where(wave > N // 2, wave - N, wave)
    other = jnp.where(device == SPECIAL, N // 2, wave)
    scale = 2.0 * math.pi / N
    scaled, scaled_other = scale * wave.astype(jnp.float32), scale * other.astype(jnp.float32)
    part = lax.broadcasted_iota(jnp.int32, (64, 128), 1) // 16 % 2
    square = jnp.where(part == 0, scaled * scaled, scaled_other * scaled_other)
    for s in both:
        set_damping(rates, plain, square, damping, s)

    slabs = [[(x // 2 + 1 - h) % 2 * 4 + j for j in range(4)] for h in both]

    def back_to_lines(s, h):
        for w in slabs[h]:
            lines_back = from_spectrum(damped, back, last, plain, w)
            returned[s, pl.ds(4 * w, 4)] = lines_back.reshape(4, 16, 128)

    for h in both:
        a2[h]()
        for w in slabs[h]:
            to_spectrum(lines, first, into, plain, spectrum, 0, w)
    diffuse(spectrum, rates, damping, damped, 0)
    a3, b3, a4, b4 = [], [], [], []
    for h in both:
        back_to_lines(0, h)
        a3.append(over_column(returned.at[0], middle_back.at[0], 8 + h, half_x[h], 16, both))
    for h in both:
        b2[h]()
    for w in range(WALLS):
        to_spectrum(lines, first, into, plain, spectrum, 1, w)
    diffuse(spectrum, rates, damping, damped, 1)
    for h in both:
        back_to_lines(1, h)
        for half in both:
            to_planes(returned.at[1], middle_back.at[1], 10 + half, half_y[half], h)
    for h in both:
        src, dst = returned.at[1], middle_back.at[1]
        done.append(await_block(src, dst, send_sem.at[10 + h], PLANE - 1, 8))
        b3.append(await_block(src, dst, recv_sem.at[10 + h], PLANE, 8))
    for h in both:
        a3[h]()
        a4.append(over_plane(middle_back.at[0], waves.at[0], 12 + h, whole_y, COLUMN, (h,)))
        b3[h]()
        b4.append(over_column(middle_back.at[1], waves.at[1], 14 + h, whole_x, PLANE, (h,)))
    for h in both:
        a4[h]()
    from_waves(waves, yi, out_ref, 0)
    for h in both:
        b4[h]()
    from_waves(waves, yi, out_ref, 1)
    pltpu.make_async_copy(rates.at[group], rates.at[group], rate_sem.at[0]).wait()
    for wait in done:
        wait()


def per_device(thermal_scalars, conductive_number):
    tables = [*y_tables(), *x_tables()]
    arrays = [jnp.asarray(t) for t in tables]
    block = pltpu.VMEM((2, PLANE, COLUMN, 128), jnp.float32)
    cube = pltpu.VMEM((2, WALLS, 64, 128), jnp.float32)
    far = pl.BlockSpec(memory_space=pltpu.HBM)
    loaded = [pltpu.VMEM(v.shape, v.dtype) for v in (thermal_scalars, *arrays)]
    result = pl.pallas_call(
        kernel,
        out_shape=jax.ShapeDtypeStruct(thermal_scalars.shape, jnp.float32),
        in_specs=[far, pl.BlockSpec(memory_space=pltpu.SMEM)] + [far] * 7,
        out_specs=pl.BlockSpec(memory_space=pltpu.VMEM),
        scratch_shapes=[
            *loaded,
            block, block, block, cube, pltpu.VMEM((WALLS, 64, 128), jnp.float32), cube,
            pltpu.VMEM((WALLS, 2, 8, 128), jnp.float32),
            block, block, block,
            pltpu.SemaphoreType.DMA((9,)), pltpu.SemaphoreType.DMA((16,)),
            pltpu.SemaphoreType.DMA((16,)), pltpu.SemaphoreType.DMA((2,)),
        ],
        compiler_params=pltpu.CompilerParams(
            collective_id=0, has_side_effects=True, vmem_limit_bytes=VMEM_LIMIT
        ),
    )(thermal_scalars, conductive_number, *arrays)
    return result * (2.0 / (N * N))


def solution(mesh):
    return jax.shard_map(
        per_device,
        mesh=mesh,
        in_specs=(P(None, "wall", "row", None), P(None, "wall")),
        out_specs=P(None, "wall", "row", None),
        check_vma=False,
    )
```

```python
import functools
import math

import jax
import jax.numpy as jnp
import numpy as np
from jax import lax
from jax.experimental import pallas as pl
from jax.experimental.pallas import tpu as pltpu
from jax.sharding import PartitionSpec as P

STEPS = 3
MESH = pl.DeviceIdType.MESH
N = 1024
COLUMN = 16
PLANE = 32
WALLS = 8
SPECIAL = 384
HALF = math.sqrt(0.5)
VMEM_LIMIT = 54400 << 10


def halves(table):
    table = np.asarray(table, np.float32)
    high = table.astype(jnp.bfloat16)
    low = (table - high.astype(np.float32)).astype(jnp.bfloat16)
    return np.stack([high, low])


def y_tables():
    b = np.arange(128)[None, :]
    m = np.arange(128)[:, None]
    forward, inverse = [], []
    for n in (1, 2, 3):
        angle = 2 * np.pi * ((b * (8 * m + n)) % N) / N
        c, s = np.cos(angle), np.sin(angle)
        forward.append(np.concatenate([c, s], 1))
        inverse.append(np.block([[c, s], [-s, c]]))
    m = m[:64]
    zero = 2 * np.pi * ((b * 8 * m) % N) / N
    four = 2 * np.pi * ((b * (8 * m + 4)) % N) / N
    c0, s0, c4, s4 = np.cos(zero), np.sin(zero), np.cos(four), np.sin(four)
    flip = np.where(b % 2 == 0, 1.0, -1.0)
    s0[:1] = -flip
    forward.append(np.block([[c0, s0], [c4, s4]]))
    c0[:1] *= 0.5
    s0[:1] *= 0.5
    none = np.zeros_like(c0)
    inverse.append(np.block([[c0, none], [none, c4], [-s0, none], [none, -s4]]))
    return np.stack(forward), np.stack(inverse)


def x_tables():
    n = np.arange(64)
    angle = 2 * np.pi * ((n[:, None] * n[None, :]) % 64) / 64
    c, s = np.cos(angle), np.sin(angle)
    first = np.concatenate([c, s], 0)
    last = np.concatenate([c, s], 1)
    i = np.arange(16)
    small = 2 * np.pi * ((i[:, None] * i[None, :]) % 16) / 16
    c, s = np.cos(small), np.sin(small)
    into = np.zeros((2, 2, 4, 16, 4, 2, 16))
    back = np.zeros((4, 2, 16, 2, 2, 4, 16))
    for part in range(2):
        for z in range(4):
            into[0, part, z, :, z, part] = c + s
            into[1, part, z, :, z, part] = c - s
            back[z, part, :, 0, part, z] = c + s
            back[z, part, :, 1, part, z] = c - s
    into, back = into.reshape(256, 128), back.reshape(128, 256)
    lane = np.arange(128)
    turn = 2 * np.pi * (n[:, None] * (lane % 16)[None, :]) / N
    return first, last, into, back, np.cos(turn), np.sin(turn)


def packed_tables():
    forward, inverse = y_tables()
    first, last, into, back, cos, sin = x_tables()
    packed = np.zeros((2, 1664, 256), jnp.bfloat16)
    packed[:, :1024] = halves(inverse.reshape(1024, 256))
    for table, place in ((back, BACK), (into, INTO), (last, LAST), (first, FIRST)):
        packed[(slice(None), *place)] = halves(table)
    for j, table in enumerate((cos, sin)):
        rest = table.astype(np.float32)
        for i in range(3):
            term = rest.astype(jnp.bfloat16)
            packed[(j, *turn_place(i))] = term
            rest = rest - term.astype(np.float32)
    return halves(forward), packed


def turn_place(i):
    return slice(1408 + 64 * i, 1472 + 64 * i), slice(0, 128)


BACK = slice(1024, 1152), slice(0, 256)
INTO = slice(1152, 1408), slice(0, 128)
LAST = slice(1152, 1216), slice(128, 256)
FIRST = slice(1216, 1344), slice(128, 192)


def split(value):
    high = value.astype(jnp.bfloat16)
    return high, (value - high.astype(jnp.float32)).astype(jnp.bfloat16)


def product(left, right, dims):
    dot = functools.partial(
        lax.dot_general, dimension_numbers=(dims, ((), ())), preferred_element_type=jnp.float32
    )
    return dot(left[0], right[0]) + (dot(left[0], right[1]) + dot(left[1], right[0]))


def pair(ref, *index):
    return ref[(0, *index)], ref[(1, *index)]


def to_waves(field, table, out, s):
    f = [field[:, 128 * a : 128 * a + 128] for a in range(8)]
    s04, d04, s26, d26 = f[0] + f[4], f[0] - f[4], f[2] + f[6], f[2] - f[6]
    s15, d15, s37, d37 = f[1] + f[5], f[1] - f[5], f[3] + f[7], f[3] - f[7]
    even, odd = s04 + s26, s15 + s37
    less, more = HALF * (d15 - d37), HALF * (d15 + d37)
    none = jnp.zeros_like(even)
    parts = [
        (d04 + less, -d26 - more),
        (s04 - s26, s37 - s15),
        (d04 - less, d26 - more),
    ]
    for j, (re, im) in enumerate(parts):
        both = jnp.concatenate(
            [jnp.concatenate([re, im], 1), jnp.concatenate([im, -re], 1)], 0
        )
        waves = product(pair(table, j), split(both), ((1,), (1,)))
        out[s, 8 * j : 8 * j + 8] = waves.reshape(8, 16, 128)
    for j, re in enumerate((even + odd, even - odd)):
        both = jnp.concatenate(
            [jnp.concatenate([re, none], 1), jnp.concatenate([none, -re], 1)], 0
        )
        rows = slice(64 * j, 64 * j + 64)
        waves = product(pair(table, 3, rows), split(both), ((1,), (1,)))
        out[s, 24 + 4 * j : 28 + 4 * j] = waves.reshape(4, 16, 128)


def from_waves(waves, table, out, s):
    u = []
    for j in range(4):
        lines = waves[s, 8 * j : 8 * j + 8].reshape(128, 128).T
        both = jnp.concatenate([lines[:64], lines[64:]], 1)
        u.append(product(split(both), pair(table, slice(256 * j, 256 * j + 256)), ((1,), (0,))))
    (re1, im1), (re2, im2), (re3, im3), (z0, z4) = [(v[:, :128], v[:, 128:]) for v in u]
    plus, minus = z0 + z4, z0 - z4
    even = [plus + re2, minus - im2, plus - re2, minus + im2]
    odd = [
        re1 + re3,
        HALF * ((re1 - im1) - (re3 + im3)),
        im3 - im1,
        HALF * ((re3 - im3) - (re1 + im1)),
    ]
    for a in range(4):
        out[s, :, :, 128 * a : 128 * a + 128] = (even[a] + odd[a]).reshape(4, 16, 128)
        out[s, :, :, 128 * a + 512 : 128 * a + 640] = (even[a] - odd[a]).reshape(4, 16, 128)


def to_spectrum(lines, tables, plain, out, s, w):
    cos, sin = plain[0], plain[1]
    block = lines[s, pl.ds(4 * w, 4)].reshape(64, 128)
    both = product(pair(tables, *FIRST), split(block), ((1,), (0,)))
    c, t = both[:64], both[64:]
    turned = jnp.concatenate([c * cos - t * sin, c * sin + t * cos], 1)
    out[s, w] = product(split(turned), pair(tables, *INTO), ((1,), (0,)))


def set_damping(rates, square, out, s):
    for w in range(WALLS):
        rate = jnp.concatenate([rates[w, s]] * 8, 0)
        out[s, w] = jnp.exp(-rate * square)


def diffuse(spectrum, rates, damping, out, s):
    lane = lax.broadcasted_iota(jnp.int32, (64, 128), 1)
    low, high = lane < 32, lane >= 96
    none = jnp.zeros((64, 128), jnp.float32)
    f = [spectrum[s, w] for w in range(WALLS)]
    for step in range(STEPS):
        new = []
        for w in range(WALLS):
            above = f[w + 1] if w + 1 < WALLS else none
            below = f[w - 1] if w else none
            up = pltpu.roll(jnp.where(low, above, f[w]), 96, 1)
            down = pltpu.roll(jnp.where(high, below, f[w]), 32, 1)
            rate = jnp.concatenate([rates[w, s]] * 8, 0)
            new.append(damping[s, w] * (f[w] + rate * (up + down - 2.0 * f[w])))
        f = new
    for w in range(WALLS):
        out[w] = f[w]


def from_spectrum(spectrum, tables, plain, w):
    cos, sin = plain[0], plain[1]
    both = product(split(spectrum[w]), pair(tables, *BACK), ((1,), (0,)))
    value, turned = both[:, :128], both[:, 128:]
    stacked = jnp.concatenate([value * cos + turned * sin, turned * cos - value * sin], 0)
    return product(pair(tables, *LAST), split(stacked), ((1,), (0,)))


def kernel(
    x_hbm, rate_ref, yf_hbm, tables_hbm, out_ref, x_ref, yf, tables, plain,
    sent, middle, lines, spectrum, damped, damping, rates,
    returned, middle_back, waves, load_sem, send_sem, recv_sem, rate_sem,
):
    wall, row = lax.axis_index("wall"), lax.axis_index("row")
    low, column = row // COLUMN, row % COLUMN
    plane = wall * 4 + low
    device = wall * 64 + row
    x, z, y, core = plane // 8, plane % 8, column // 2, column % 2

    loads = [
        (x_hbm.at[0], x_ref.at[0]), (yf_hbm, yf), (x_hbm.at[1], x_ref.at[1]), (tables_hbm, tables),
    ]
    loads = [pltpu.make_async_copy(*refs, load_sem.at[k]) for k, refs in enumerate(loads)]
    for load in loads[:3]:
        load.start()

    def column_id(c):
        return wall, low * COLUMN + c

    def plane_id(p):
        return p // 4, lax.rem(p, 4) * COLUMN + column

    def column_peer(h, i):
        half = (y // 4 + 1 - h) % 2
        return (half * 4 + (y + i // 2) % 4) * 2 + (core + i) % 2

    far_x = [(x // 2 + 1) % 2 * 2 + (x + q) % 2 for q in range(2)]

    def far_peer(q, i):
        return far_x[q] * 8 + (z + i) % 8

    def near_peer(i):
        return (x // 2 * 2 + (x + i // 8) % 2) * 8 + (z + i) % 8

    barrier = pltpu.get_barrier_semaphore()

    def greet(to):
        pl.semaphore_signal(barrier, inc=1, device_id=to, device_id_type=MESH)

    for q in range(2):
        for i in (4, 3, 5, 2, 6, 1, 7, 0):
            greet(plane_id(far_peer(q, i)))
    for i in range(8):
        greet(column_id(column_peer(0, i)))
    for i in range(15, 0, -1):
        greet(plane_id(near_peer(i)))
    for i in range(1, 8):
        greet(column_id(column_peer(1, i)))

    loads[3].start()

    half_x = [pl.ds(pl.multiple_of((x // 2 + 1 - h) % 2 * 16, 16), 16) for h in range(2)]
    quarter_x = [pl.ds(pl.multiple_of(far_x[q] * 8, 8), 8) for q in range(2)]
    half_y = [pl.ds(pl.multiple_of((y // 4 + 1 - h) % 2 * 8, 8), 8) for h in range(2)]
    done = []

    def remote(src, dst, k, to):
        pltpu.make_async_remote_copy(
            src_ref=src, dst_ref=dst, send_sem=send_sem.at[k], recv_sem=recv_sem.at[k],
            device_id=to, device_id_type=MESH,
        ).start()

    def await_block(src, dst, sem, rows, columns):
        part = (pl.ds(0, rows), pl.ds(0, columns))
        return pltpu.make_async_copy(src.at[part], dst.at[part], sem).wait

    def to_column(src, dst, k, xs, h):
        if h:
            pltpu.make_async_copy(src.at[xs, column], dst.at[xs, column], recv_sem.at[k]).start()

        @pl.loop(h, 8)
        def _(i):
            c = column_peer(h, i)
            remote(src.at[xs, c], dst.at[xs, column], k, column_id(c))

    def expect(src, dst, k, rows, columns, out_rows, out_columns):
        done.append(await_block(src, dst, send_sem.at[k], out_rows, out_columns))
        return await_block(src, dst, recv_sem.at[k], rows, columns)

    def far_first(src, mid, k, q):
        for h in range(2):
            to_column(src, mid, k + q, quarter_x[q], h)
        return expect(src, mid, k + q, 8, 16, 8, 15)

    def far_second(mid, dst, k, q):
        @pl.loop(0, 8)
        def _(i):
            p = far_peer(q, i)
            remote(mid.at[p], dst.at[plane], k + 2, plane_id(p))

        return expect(mid, dst, k + 2, 16, 16, 16, 16) if q else None

    def near_first(src, mid, k, q):
        ys = half_y[q]
        pltpu.make_async_copy(
            src.at[plane, ys], mid.at[plane, ys], recv_sem.at[k + 3 + q]
        ).start()

        @pl.loop(1, 16)
        def _(i):
            p = near_peer(i)
            remote(src.at[p, ys], mid.at[plane, ys], k + 3 + q, plane_id(p))

        return expect(src, mid, k + 3 + q, 16, 8, 15, 8)

    def near_second(mid, dst, k, q):
        to_column(mid, dst, k + 5, half_x[1], q)
        return expect(mid, dst, k + 5, 16, 16, 16, 15) if q else None

    zone = lax.broadcasted_iota(jnp.int32, (8, 128), 1) // 32
    for s in range(2):
        value = jnp.full((8, 128), rate_ref[s, 0], jnp.float32)
        for j in range(1, 4):
            value = jnp.where(zone == j, rate_ref[s, j], value)
        rates[wall, s] = value
    for s in range(2):
        if s == 0:
            loads[1].wait()
        loads[2 * s].wait()
        to_waves(x_ref[s].reshape(64, N), yf, sent, s)
    pl.semaphore_wait(barrier, PLANE + COLUMN - 2)

    both = (0, 1)
    first_steps = []
    for s in both:
        for q in both:
            first_steps.append(far_first(sent.at[s], middle.at[s], 6 * s, q))
            first_steps.append(near_first(sent.at[s], middle.at[s], 6 * s, q))

    @pl.loop(1, WALLS)
    def _(i):
        pltpu.make_async_remote_copy(
            src_ref=rates.at[wall], dst_ref=rates.at[wall],
            send_sem=rate_sem.at[0], recv_sem=rate_sem.at[1],
            device_id=(lax.rem(wall + i, WALLS), row), device_id_type=MESH,
        ).start()

    def second_steps(waits, mid, dst, k):
        for q in both:
            waits[2 * q]()
            far = far_second(mid, dst, k, q)
            waits[2 * q + 1]()
            near = near_second(mid, dst, k, q)
        return far, near

    arrived = [
        second_steps(first_steps[4 * s : 4 * s + 4], middle.at[s], lines.at[s], 6 * s)
        for s in both
    ]

    group = pl.ds(0, WALLS - 1)
    pltpu.make_async_copy(rates.at[group], rates.at[group], rate_sem.at[1]).wait()
    loads[3].wait()
    for j in range(2):
        terms = [tables[(j, *turn_place(i))].astype(jnp.float32) for i in range(3)]
        plain[j] = terms[0] + (terms[1] + terms[2])
    group_of, m = device // 128, device % 128
    wave = jnp.where(group_of < 3, 8 * m + group_of + 1, 8 * lax.rem(m, 64) + 4 * (m // 64))
    wave = jnp.where(wave > N // 2, wave - N, wave)
    other = jnp.where(device == SPECIAL, N // 2, wave)
    scale = 2.0 * math.pi / N
    scaled, scaled_other = scale * wave.astype(jnp.float32), scale * other.astype(jnp.float32)
    lane = lax.broadcasted_iota(jnp.int32, (64, 128), 1)
    square = jnp.where(lane // 16 % 2 == 0, scaled * scaled, scaled_other * scaled_other)
    wave_x = lax.broadcasted_iota(jnp.int32, (64, 128), 0) + 64 * (lane % 16)
    wave_x = scale * jnp.where(wave_x > N // 2, wave_x - N, wave_x).astype(jnp.float32)
    square = square + wave_x * wave_x
    for s in both:
        set_damping(rates, square, damping, s)

    slabs = [[(x // 2 + 1 - h) % 2 * 4 + j for j in range(4)] for h in both]

    def back_to_lines(s, h):
        for w in slabs[h]:
            lines_back = from_spectrum(damped, tables, plain, w)
            returned[s, pl.ds(4 * w, 4)] = lines_back.reshape(4, 16, 128)

    first_steps = []
    for s in both:
        for h in both:
            arrived[s][h]()
            for w in slabs[h]:
                to_spectrum(lines, tables, plain, spectrum, s, w)
        diffuse(spectrum, rates, damping, damped, s)
        for h, send in enumerate((far_first, near_first)):
            back_to_lines(s, h)
            for q in both:
                first_steps.append(send(returned.at[s], middle_back.at[s], 12 + 6 * s, q))
    for s in both:
        far0, far1, near0, near1 = first_steps[4 * s : 4 * s + 4]
        waits = far0, near0, far1, near1
        arrived[s] = second_steps(waits, middle_back.at[s], waves.at[s], 12 + 6 * s)
    for s in both:
        for wait in arrived[s]:
            wait()
        from_waves(waves, tables, out_ref, s)
    pltpu.make_async_copy(rates.at[group], rates.at[group], rate_sem.at[0]).wait()
    for wait in done:
        wait()


def per_device(thermal_scalars, conductive_number):
    arrays = [jnp.asarray(table) for table in packed_tables()]
    block = pltpu.VMEM((2, PLANE, COLUMN, 128), jnp.float32)
    cube = pltpu.VMEM((2, WALLS, 64, 128), jnp.float32)
    far = pl.BlockSpec(memory_space=pltpu.HBM)
    loaded = [pltpu.VMEM(v.shape, v.dtype) for v in (thermal_scalars, *arrays)]
    result = pl.pallas_call(
        kernel,
        out_shape=jax.ShapeDtypeStruct(thermal_scalars.shape, jnp.float32),
        in_specs=[far, pl.BlockSpec(memory_space=pltpu.SMEM)] + [far] * 2,
        out_specs=pl.BlockSpec(memory_space=pltpu.VMEM),
        scratch_shapes=[
            *loaded, pltpu.VMEM((2, 64, 128), jnp.float32),
            block, block, block, cube, pltpu.VMEM((WALLS, 64, 128), jnp.float32), cube,
            pltpu.VMEM((WALLS, 2, 8, 128), jnp.float32),
            block, block, block,
            pltpu.SemaphoreType.DMA((4,)), pltpu.SemaphoreType.DMA((24,)),
            pltpu.SemaphoreType.DMA((24,)), pltpu.SemaphoreType.DMA((2,)),
        ],
        compiler_params=pltpu.CompilerParams(
            collective_id=0, has_side_effects=True, vmem_limit_bytes=VMEM_LIMIT
        ),
    )(thermal_scalars, conductive_number, *arrays)
    return result * (2.0 / (N * N))


def solution(mesh):
    return jax.shard_map(
        per_device,
        mesh=mesh,
        in_specs=(P(None, "wall", "row", None), P(None, "wall")),
        out_specs=P(None, "wall", "row", None),
        check_vma=False,
    )
```

```python
import functools
import math

import jax
import jax.numpy as jnp
import numpy as np
from jax import lax
from jax.experimental import pallas as pl
from jax.experimental.pallas import tpu as pltpu
from jax.sharding import PartitionSpec as P

STEPS = 3
MESH = pl.DeviceIdType.MESH
N = 1024
COLUMN = 16
PLANE = 32
WALLS = 8
SPECIAL = 384
HALF = math.sqrt(0.5)
VMEM_LIMIT = 54400 << 10


def halves(table):
    table = np.asarray(table, np.float32)
    high = table.astype(jnp.bfloat16)
    low = (table - high.astype(np.float32)).astype(jnp.bfloat16)
    return np.stack([high, low])


def y_tables():
    b = np.arange(128)[None, :]
    m = np.arange(128)[:, None]
    forward, inverse = [], []
    for n in (1, 2, 3):
        angle = 2 * np.pi * ((b * (8 * m + n)) % N) / N
        c, s = np.cos(angle), np.sin(angle)
        forward.append(np.concatenate([c, s], 1))
        inverse.append(np.block([[c, s], [-s, c]]))
    m = m[:64]
    zero = 2 * np.pi * ((b * 8 * m) % N) / N
    four = 2 * np.pi * ((b * (8 * m + 4)) % N) / N
    c0, s0, c4, s4 = np.cos(zero), np.sin(zero), np.cos(four), np.sin(four)
    flip = np.where(b % 2 == 0, 1.0, -1.0)
    s0[:1] = -flip
    forward.append(np.block([[c0, s0], [c4, s4]]))
    c0[:1] *= 0.5
    s0[:1] *= 0.5
    none = np.zeros_like(c0)
    inverse.append(np.block([[c0, none], [none, c4], [-s0, none], [none, -s4]]))
    return np.stack(forward), np.stack(inverse)


def x_tables():
    n = np.arange(64)
    angle = 2 * np.pi * ((n[:, None] * n[None, :]) % 64) / 64
    c, s = np.cos(angle), np.sin(angle)
    first = np.concatenate([c, s], 0)
    last = np.concatenate([c, s], 1)
    i = np.arange(16)
    small = 2 * np.pi * ((i[:, None] * i[None, :]) % 16) / 16
    c, s = np.cos(small), np.sin(small)
    into = np.zeros((2, 2, 4, 16, 4, 2, 16))
    back = np.zeros((4, 2, 16, 2, 2, 4, 16))
    for part in range(2):
        for z in range(4):
            into[0, part, z, :, z, part] = c + s
            into[1, part, z, :, z, part] = c - s
            back[z, part, :, 0, part, z] = c + s
            back[z, part, :, 1, part, z] = c - s
    into, back = into.reshape(256, 128), back.reshape(128, 256)
    lane = np.arange(128)
    turn = 2 * np.pi * (n[:, None] * (lane % 16)[None, :]) / N
    return first, last, into, back, np.cos(turn), np.sin(turn)


def packed_tables():
    forward, inverse = y_tables()
    first, last, into, back, cos, sin = x_tables()
    packed = np.zeros((2, 1664, 256), jnp.bfloat16)
    packed[:, :1024] = halves(inverse.reshape(1024, 256))
    for table, place in ((back, BACK), (into, INTO), (last, LAST), (first, FIRST)):
        packed[(slice(None), *place)] = halves(table)
    for j, table in enumerate((cos, sin)):
        rest = table.astype(np.float32)
        for i in range(3):
            term = rest.astype(jnp.bfloat16)
            packed[(j, *turn_place(i))] = term
            rest = rest - term.astype(np.float32)
    return halves(forward), packed


def turn_place(i):
    return slice(1408 + 64 * i, 1472 + 64 * i), slice(0, 128)


BACK = slice(1024, 1152), slice(0, 256)
INTO = slice(1152, 1408), slice(0, 128)
LAST = slice(1152, 1216), slice(128, 256)
FIRST = slice(1216, 1344), slice(128, 192)


def split(value):
    high = value.astype(jnp.bfloat16)
    return high, (value - high.astype(jnp.float32)).astype(jnp.bfloat16)


def product(left, right, dims):
    dot = functools.partial(
        lax.dot_general, dimension_numbers=(dims, ((), ())), preferred_element_type=jnp.float32
    )
    return dot(left[0], right[0]) + (dot(left[0], right[1]) + dot(left[1], right[0]))


def pair(ref, *index):
    return ref[(0, *index)], ref[(1, *index)]


def to_waves(field, table, out, s):
    f = [field[:, 128 * a : 128 * a + 128] for a in range(8)]
    s04, d04, s26, d26 = f[0] + f[4], f[0] - f[4], f[2] + f[6], f[2] - f[6]
    s15, d15, s37, d37 = f[1] + f[5], f[1] - f[5], f[3] + f[7], f[3] - f[7]
    even, odd = s04 + s26, s15 + s37
    less, more = HALF * (d15 - d37), HALF * (d15 + d37)
    none = jnp.zeros_like(even)
    parts = [
        (d04 + less, -d26 - more),
        (s04 - s26, s37 - s15),
        (d04 - less, d26 - more),
    ]
    for j, (re, im) in enumerate(parts):
        both = jnp.concatenate(
            [jnp.concatenate([re, im], 1), jnp.concatenate([im, -re], 1)], 0
        )
        waves = product(pair(table, j), split(both), ((1,), (1,)))
        out[s, 8 * j : 8 * j + 8] = waves.reshape(8, 16, 128)
    for j, re in enumerate((even + odd, even - odd)):
        both = jnp.concatenate(
            [jnp.concatenate([re, none], 1), jnp.concatenate([none, -re], 1)], 0
        )
        rows = slice(64 * j, 64 * j + 64)
        waves = product(pair(table, 3, rows), split(both), ((1,), (1,)))
        out[s, 24 + 4 * j : 28 + 4 * j] = waves.reshape(4, 16, 128)


def from_waves(waves, table, out, s):
    u = []
    for j in range(4):
        lines = waves[s, 8 * j : 8 * j + 8].reshape(128, 128).T
        both = jnp.concatenate([lines[:64], lines[64:]], 1)
        u.append(product(split(both), pair(table, slice(256 * j, 256 * j + 256)), ((1,), (0,))))
    (re1, im1), (re2, im2), (re3, im3), (z0, z4) = [(v[:, :128], v[:, 128:]) for v in u]
    plus, minus = z0 + z4, z0 - z4
    even = [plus + re2, minus - im2, plus - re2, minus + im2]
    odd = [
        re1 + re3,
        HALF * ((re1 - im1) - (re3 + im3)),
        im3 - im1,
        HALF * ((re3 - im3) - (re1 + im1)),
    ]
    for a in range(4):
        out[s, :, :, 128 * a : 128 * a + 128] = (even[a] + odd[a]).reshape(4, 16, 128)
        out[s, :, :, 128 * a + 512 : 128 * a + 640] = (even[a] - odd[a]).reshape(4, 16, 128)


def to_spectrum(lines, tables, plain, out, s, w):
    cos, sin = plain[0], plain[1]
    block = lines[s, pl.ds(4 * w, 4)].reshape(64, 128)
    both = product(pair(tables, *FIRST), split(block), ((1,), (0,)))
    c, t = both[:64], both[64:]
    turned = jnp.concatenate([c * cos - t * sin, c * sin + t * cos], 1)
    out[s, w] = product(split(turned), pair(tables, *INTO), ((1,), (0,)))


def set_damping(rates, square, out, s):
    for w in range(WALLS):
        rate = jnp.concatenate([rates[w, s]] * 8, 0)
        out[s, w] = jnp.exp(-rate * square)


def diffuse(spectrum, rates, damping, out, s):
    lane = lax.broadcasted_iota(jnp.int32, (64, 128), 1)
    low, high = lane < 32, lane >= 96
    none = jnp.zeros((64, 128), jnp.float32)
    f = [spectrum[s, w] for w in range(WALLS)]
    for step in range(STEPS):
        new = []
        for w in range(WALLS):
            above = f[w + 1] if w + 1 < WALLS else none
            below = f[w - 1] if w else none
            up = pltpu.roll(jnp.where(low, above, f[w]), 96, 1)
            down = pltpu.roll(jnp.where(high, below, f[w]), 32, 1)
            rate = jnp.concatenate([rates[w, s]] * 8, 0)
            new.append(damping[s, w] * (f[w] + rate * (up + down - 2.0 * f[w])))
        f = new
    for w in range(WALLS):
        out[w] = f[w]


def from_spectrum(spectrum, tables, plain, w):
    cos, sin = plain[0], plain[1]
    both = product(split(spectrum[w]), pair(tables, *BACK), ((1,), (0,)))
    value, turned = both[:, :128], both[:, 128:]
    stacked = jnp.concatenate([value * cos + turned * sin, turned * cos - value * sin], 0)
    return product(pair(tables, *LAST), split(stacked), ((1,), (0,)))


def kernel(
    x_hbm, rate_ref, yf_hbm, tables_hbm, out_ref, x_ref, yf, tables, plain,
    sent, middle, lines, spectrum, damped, damping, rates,
    returned, middle_back, waves, load_sem, send_sem, recv_sem, rate_sem,
):
    wall, row = lax.axis_index("wall"), lax.axis_index("row")
    low, column = row // COLUMN, row % COLUMN
    plane = wall * 4 + low
    device = wall * 64 + row
    x, z, y, core = plane // 8, plane % 8, column // 2, column % 2

    loads = [
        (x_hbm.at[0], x_ref.at[0]), (yf_hbm, yf), (x_hbm.at[1], x_ref.at[1]), (tables_hbm, tables),
    ]
    loads = [pltpu.make_async_copy(*refs, load_sem.at[k]) for k, refs in enumerate(loads)]
    for load in loads[:3]:
        load.start()

    def column_id(c):
        return wall, low * COLUMN + c

    def plane_id(p):
        return p // 4, lax.rem(p, 4) * COLUMN + column

    def column_peer(h, i):
        half = (y // 4 + 1 - h) % 2
        return (half * 4 + (y + i // 2) % 4) * 2 + (core + i) % 2

    far_x = [(x // 2 + 1) % 2 * 2 + (x + q) % 2 for q in range(2)]

    def far_peer(q, i):
        return far_x[q] * 8 + (z + i) % 8

    def near_peer(i):
        return (x // 2 * 2 + (x + i // 8) % 2) * 8 + (z + i) % 8

    def farthest(t):
        return (4 + (t + 1) // 2 * (1 - 2 * (t % 2))) % 8

    barrier = pltpu.get_barrier_semaphore()

    def greet(to):
        pl.semaphore_signal(barrier, inc=1, device_id=to, device_id_type=MESH)

    for q in range(2):
        for i in (4, 3, 5, 2, 6, 1, 7, 0):
            greet(plane_id(far_peer(q, i)))
    for i in range(8):
        greet(column_id(column_peer(0, i)))
    for i in range(15, 0, -1):
        greet(plane_id(near_peer(i)))
    for i in range(1, 8):
        greet(column_id(column_peer(1, i)))

    loads[3].start()

    half_x = [pl.ds(pl.multiple_of((x // 2 + 1 - h) % 2 * 16, 16), 16) for h in range(2)]
    quarter_x = [pl.ds(pl.multiple_of(far_x[q] * 8, 8), 8) for q in range(2)]
    half_y = [pl.ds(pl.multiple_of((y // 4 + 1 - h) % 2 * 8, 8), 8) for h in range(2)]
    done = []

    def remote(src, dst, k, to):
        pltpu.make_async_remote_copy(
            src_ref=src, dst_ref=dst, send_sem=send_sem.at[k], recv_sem=recv_sem.at[k],
            device_id=to, device_id_type=MESH,
        ).start()

    def await_block(src, dst, sem, rows, columns):
        part = (pl.ds(0, rows), pl.ds(0, columns))
        return pltpu.make_async_copy(src.at[part], dst.at[part], sem).wait

    def to_column(src, dst, k, xs, h):
        if h:
            pltpu.make_async_copy(src.at[xs, column], dst.at[xs, column], recv_sem.at[k]).start()

        @pl.loop(0, 8 - h)
        def _(t):
            c = column_peer(h, 7 - t if h else t)
            remote(src.at[xs, c], dst.at[xs, column], k, column_id(c))

    def expect(src, dst, k, rows, columns, out_rows, out_columns):
        done.append(await_block(src, dst, send_sem.at[k], out_rows, out_columns))
        return await_block(src, dst, recv_sem.at[k], rows, columns)

    def far_first(src, mid, k, q):
        xs = quarter_x[q]
        pltpu.make_async_copy(src.at[xs, column], mid.at[xs, column], recv_sem.at[k + q]).start()

        def send(t, other):
            c = (y + farthest(t)) % 8 * 2 + (core + other) % 2
            remote(src.at[xs, c], mid.at[xs, column], k + q, column_id(c))

        @pl.loop(0, 7)
        def _(t):
            send(t, 0)
            send(t, 1)

        send(7, 1)
        return expect(src, mid, k + q, 8, 16, 8, 15)

    def far_second(mid, dst, k, q):
        @pl.loop(0, 8)
        def _(i):
            p = far_peer(q, farthest(i))
            remote(mid.at[p], dst.at[plane], k + 2, plane_id(p))

        return expect(mid, dst, k + 2, 16, 16, 16, 16) if q else None

    def near_first(src, mid, k, q):
        ys = half_y[q]
        pltpu.make_async_copy(
            src.at[plane, ys], mid.at[plane, ys], recv_sem.at[k + 3 + q]
        ).start()

        def send(i):
            p = near_peer(i)
            remote(src.at[p, ys], mid.at[plane, ys], k + 3 + q, plane_id(p))

        @pl.loop(0, 7)
        def _(t):
            send(8 + farthest(t))
            send(farthest(t))

        send(8)

        return expect(src, mid, k + 3 + q, 16, 8, 15, 8)

    def near_second(mid, dst, k, q):
        to_column(mid, dst, k + 5, half_x[1], q)
        return expect(mid, dst, k + 5, 16, 16, 16, 15) if q else None

    zone = lax.broadcasted_iota(jnp.int32, (8, 128), 1) // 32
    for s in range(2):
        value = jnp.broadcast_to(rate_ref[s : s + 1, 0:1], (8, 128))
        for j in range(1, 4):
            value = jnp.where(zone == j, rate_ref[s : s + 1, j : j + 1], value)
        rates[wall, s] = value
    for s in range(2):
        if s == 0:
            loads[1].wait()
        loads[2 * s].wait()
        to_waves(x_ref[s].reshape(64, N), yf, sent, s)
    pl.semaphore_wait(barrier, PLANE + COLUMN - 2)

    both = (0, 1)
    first_steps = []
    for s in both:
        for q in both:
            near = near_first(sent.at[s], middle.at[s], 6 * s, q)
            first_steps.append(far_first(sent.at[s], middle.at[s], 6 * s, q))
            first_steps.append(near)

    @pl.loop(1, WALLS)
    def _(i):
        pltpu.make_async_remote_copy(
            src_ref=rates.at[wall], dst_ref=rates.at[wall],
            send_sem=rate_sem.at[0], recv_sem=rate_sem.at[1],
            device_id=(lax.rem(wall + i, WALLS), row), device_id_type=MESH,
        ).start()

    def second_steps(waits, mid, dst, k):
        for q in both:
            waits[2 * q + 1]()
            near = near_second(mid, dst, k, q)
            waits[2 * q]()
            far = far_second(mid, dst, k, q)
        return far, near

    arrived = [
        second_steps(first_steps[4 * s : 4 * s + 4], middle.at[s], lines.at[s], 6 * s)
        for s in both
    ]

    group = pl.ds(0, WALLS - 1)
    pltpu.make_async_copy(rates.at[group], rates.at[group], rate_sem.at[1]).wait()
    loads[3].wait()
    for j in range(2):
        terms = [tables[(j, *turn_place(i))].astype(jnp.float32) for i in range(3)]
        plain[j] = terms[0] + (terms[1] + terms[2])
    group_of, m = device // 128, device % 128
    wave = jnp.where(group_of < 3, 8 * m + group_of + 1, 8 * lax.rem(m, 64) + 4 * (m // 64))
    wave = jnp.where(wave > N // 2, wave - N, wave)
    other = jnp.where(device == SPECIAL, N // 2, wave)
    scale = 2.0 * math.pi / N
    scaled, scaled_other = scale * wave.astype(jnp.float32), scale * other.astype(jnp.float32)
    lane = lax.broadcasted_iota(jnp.int32, (64, 128), 1)
    square = jnp.where(lane // 16 % 2 == 0, scaled * scaled, scaled_other * scaled_other)
    wave_x = lax.broadcasted_iota(jnp.int32, (64, 128), 0) + 64 * (lane % 16)
    wave_x = scale * jnp.where(wave_x > N // 2, wave_x - N, wave_x).astype(jnp.float32)
    square = square + wave_x * wave_x
    for s in both:
        set_damping(rates, square, damping, s)

    slabs = [[(x // 2 + 1 - h) % 2 * 4 + j for j in range(4)] for h in both]

    def back_to_lines(s, h):
        for w in slabs[h]:
            lines_back = from_spectrum(damped, tables, plain, w)
            returned[s, pl.ds(4 * w, 4)] = lines_back.reshape(4, 16, 128)

    first_steps = []
    for s in both:
        for h in both:
            arrived[s][h]()
            for w in slabs[h]:
                to_spectrum(lines, tables, plain, spectrum, s, w)
        diffuse(spectrum, rates, damping, damped, s)
        for h, send in enumerate((far_first, near_first)):
            back_to_lines(s, h)
            for q in both:
                first_steps.append(send(returned.at[s], middle_back.at[s], 12 + 6 * s, q))
    for s in both:
        far0, far1, near0, near1 = first_steps[4 * s : 4 * s + 4]
        waits = far0, near0, far1, near1
        arrived[s] = second_steps(waits, middle_back.at[s], waves.at[s], 12 + 6 * s)
    for s in both:
        for wait in arrived[s]:
            wait()
        from_waves(waves, tables, out_ref, s)
    pltpu.make_async_copy(rates.at[group], rates.at[group], rate_sem.at[0]).wait()
    for wait in done:
        wait()


def per_device(thermal_scalars, conductive_number):
    arrays = [jnp.asarray(table) for table in packed_tables()]
    block = pltpu.VMEM((2, PLANE, COLUMN, 128), jnp.float32)
    cube = pltpu.VMEM((2, WALLS, 64, 128), jnp.float32)
    far = pl.BlockSpec(memory_space=pltpu.HBM)
    loaded = [pltpu.VMEM(v.shape, v.dtype) for v in (thermal_scalars, *arrays)]
    result = pl.pallas_call(
        kernel,
        out_shape=jax.ShapeDtypeStruct(thermal_scalars.shape, jnp.float32),
        in_specs=[far, pl.BlockSpec(memory_space=pltpu.VMEM), far, far],
        out_specs=pl.BlockSpec(memory_space=pltpu.VMEM),
        scratch_shapes=[
            *loaded, pltpu.VMEM((2, 64, 128), jnp.float32),
            block, block, block, cube, pltpu.VMEM((WALLS, 64, 128), jnp.float32), cube,
            pltpu.VMEM((WALLS, 2, 8, 128), jnp.float32),
            block, block, block,
            pltpu.SemaphoreType.DMA((4,)), pltpu.SemaphoreType.DMA((24,)),
            pltpu.SemaphoreType.DMA((24,)), pltpu.SemaphoreType.DMA((2,)),
        ],
        compiler_params=pltpu.CompilerParams(
            collective_id=0, has_side_effects=True, vmem_limit_bytes=VMEM_LIMIT
        ),
    )(thermal_scalars, conductive_number, *arrays)
    return result * (2.0 / (N * N))


def solution(mesh):
    return jax.shard_map(
        per_device,
        mesh=mesh,
        in_specs=(P(None, "wall", "row", None), P(None, "wall")),
        out_specs=P(None, "wall", "row", None),
        check_vma=False,
    )
```

```python
import functools
import math

import jax
import jax.numpy as jnp
import numpy as np
from jax import lax
from jax.experimental import pallas as pl
from jax.experimental.pallas import tpu as pltpu
from jax.sharding import PartitionSpec as P

STEPS = 3
MESH = pl.DeviceIdType.MESH
N = 1024
COLUMN = 16
PLANE = 32
WALLS = 8
SPECIAL = 384
HALF = math.sqrt(0.5)
VMEM_LIMIT = 54400 << 10


def halves(table):
    table = np.asarray(table, np.float32)
    high = table.astype(jnp.bfloat16)
    low = (table - high.astype(np.float32)).astype(jnp.bfloat16)
    return np.stack([high, low])


def y_tables():
    b = np.arange(128)[None, :]
    m = np.arange(128)[:, None]
    forward, inverse = [], []
    for n in (1, 2, 3):
        angle = 2 * np.pi * ((b * (8 * m + n)) % N) / N
        c, s = np.cos(angle), np.sin(angle)
        forward.append(np.concatenate([c, s], 1))
        inverse.append(np.block([[c, s], [-s, c]]))
    m = m[:64]
    zero = 2 * np.pi * ((b * 8 * m) % N) / N
    four = 2 * np.pi * ((b * (8 * m + 4)) % N) / N
    c0, s0, c4, s4 = np.cos(zero), np.sin(zero), np.cos(four), np.sin(four)
    flip = np.where(b % 2 == 0, 1.0, -1.0)
    s0[:1] = -flip
    forward.append(np.block([[c0, s0], [c4, s4]]))
    c0[:1] *= 0.5
    s0[:1] *= 0.5
    none = np.zeros_like(c0)
    inverse.append(np.block([[c0, none], [none, c4], [-s0, none], [none, -s4]]))
    return np.stack(forward), np.stack(inverse)


def x_tables():
    n = np.arange(64)
    angle = 2 * np.pi * ((n[:, None] * n[None, :]) % 64) / 64
    c, s = np.cos(angle), np.sin(angle)
    first = np.concatenate([c, s], 0)
    last = np.concatenate([c, s], 1)
    i = np.arange(16)
    small = 2 * np.pi * ((i[:, None] * i[None, :]) % 16) / 16
    c, s = np.cos(small), np.sin(small)
    into = np.zeros((2, 2, 4, 16, 4, 2, 16))
    back = np.zeros((4, 2, 16, 2, 2, 4, 16))
    for part in range(2):
        for z in range(4):
            into[0, part, z, :, z, part] = c + s
            into[1, part, z, :, z, part] = c - s
            back[z, part, :, 0, part, z] = c + s
            back[z, part, :, 1, part, z] = c - s
    into, back = into.reshape(256, 128), back.reshape(128, 256)
    lane = np.arange(128)
    turn = 2 * np.pi * (n[:, None] * (lane % 16)[None, :]) / N
    return first, last, into, back, np.cos(turn), np.sin(turn)


def packed_tables():
    forward, inverse = y_tables()
    first, last, into, back, cos, sin = x_tables()
    packed = np.zeros((2, 1664, 256), jnp.bfloat16)
    packed[:, :1024] = halves(inverse.reshape(1024, 256))
    for table, place in ((back, BACK), (into, INTO), (last, LAST), (first, FIRST)):
        packed[(slice(None), *place)] = halves(table)
    for j, table in enumerate((cos, sin)):
        rest = table.astype(np.float32)
        for i in range(3):
            term = rest.astype(jnp.bfloat16)
            packed[(j, *turn_place(i))] = term
            rest = rest - term.astype(np.float32)
    return halves(forward), packed


def turn_place(i):
    return slice(1408 + 64 * i, 1472 + 64 * i), slice(0, 128)


BACK = slice(1024, 1152), slice(0, 256)
INTO = slice(1152, 1408), slice(0, 128)
LAST = slice(1152, 1216), slice(128, 256)
FIRST = slice(1216, 1344), slice(128, 192)


def split(value):
    high = value.astype(jnp.bfloat16)
    return high, (value - high.astype(jnp.float32)).astype(jnp.bfloat16)


def product(left, right, dims):
    dot = functools.partial(
        lax.dot_general, dimension_numbers=(dims, ((), ())), preferred_element_type=jnp.float32
    )
    return dot(left[0], right[0]) + (dot(left[0], right[1]) + dot(left[1], right[0]))


def pair(ref, *index):
    return ref[(0, *index)], ref[(1, *index)]


def to_waves(field, table, out, s):
    f = [field[:, 128 * a : 128 * a + 128] for a in range(8)]
    s04, d04, s26, d26 = f[0] + f[4], f[0] - f[4], f[2] + f[6], f[2] - f[6]
    s15, d15, s37, d37 = f[1] + f[5], f[1] - f[5], f[3] + f[7], f[3] - f[7]
    even, odd = s04 + s26, s15 + s37
    less, more = HALF * (d15 - d37), HALF * (d15 + d37)
    none = jnp.zeros_like(even)
    parts = [
        (d04 + less, -d26 - more),
        (s04 - s26, s37 - s15),
        (d04 - less, d26 - more),
    ]
    for j, (re, im) in enumerate(parts):
        both = jnp.concatenate(
            [jnp.concatenate([re, im], 1), jnp.concatenate([im, -re], 1)], 0
        )
        waves = product(pair(table, j), split(both), ((1,), (1,)))
        out[s, 8 * j : 8 * j + 8] = waves.reshape(8, 16, 128)
    for j, re in enumerate((even + odd, even - odd)):
        both = jnp.concatenate(
            [jnp.concatenate([re, none], 1), jnp.concatenate([none, -re], 1)], 0
        )
        rows = slice(64 * j, 64 * j + 64)
        waves = product(pair(table, 3, rows), split(both), ((1,), (1,)))
        out[s, 24 + 4 * j : 28 + 4 * j] = waves.reshape(4, 16, 128)


def from_waves(waves, table, out, s):
    u = []
    for j in range(4):
        lines = waves[s, 8 * j : 8 * j + 8].reshape(128, 128).T
        both = jnp.concatenate([lines[:64], lines[64:]], 1)
        u.append(product(split(both), pair(table, slice(256 * j, 256 * j + 256)), ((1,), (0,))))
    (re1, im1), (re2, im2), (re3, im3), (z0, z4) = [(v[:, :128], v[:, 128:]) for v in u]
    plus, minus = z0 + z4, z0 - z4
    even = [plus + re2, minus - im2, plus - re2, minus + im2]
    odd = [
        re1 + re3,
        HALF * ((re1 - im1) - (re3 + im3)),
        im3 - im1,
        HALF * ((re3 - im3) - (re1 + im1)),
    ]
    for a in range(4):
        out[s, :, :, 128 * a : 128 * a + 128] = (even[a] + odd[a]).reshape(4, 16, 128)
        out[s, :, :, 128 * a + 512 : 128 * a + 640] = (even[a] - odd[a]).reshape(4, 16, 128)


def to_spectrum(lines, tables, plain, out, s, w):
    cos, sin = plain[0], plain[1]
    block = lines[s, pl.ds(4 * w, 4)].reshape(64, 128)
    both = product(pair(tables, *FIRST), split(block), ((1,), (0,)))
    c, t = both[:64], both[64:]
    turned = jnp.concatenate([c * cos - t * sin, c * sin + t * cos], 1)
    out[s, w] = product(split(turned), pair(tables, *INTO), ((1,), (0,)))


def set_damping(rates, square, out, s):
    for w in range(WALLS):
        rate = jnp.concatenate([rates[w, s]] * 8, 0)
        out[s, w] = jnp.exp(-rate * square)


def diffuse(spectrum, rates, damping, out, s):
    lane = lax.broadcasted_iota(jnp.int32, (64, 128), 1)
    low, high = lane < 32, lane >= 96
    none = jnp.zeros((64, 128), jnp.float32)
    f = [spectrum[s, w] for w in range(WALLS)]
    for step in range(STEPS):
        new = []
        for w in range(WALLS):
            above = f[w + 1] if w + 1 < WALLS else none
            below = f[w - 1] if w else none
            up = pltpu.roll(jnp.where(low, above, f[w]), 96, 1)
            down = pltpu.roll(jnp.where(high, below, f[w]), 32, 1)
            rate = jnp.concatenate([rates[w, s]] * 8, 0)
            new.append(damping[s, w] * (f[w] + rate * (up + down - 2.0 * f[w])))
        f = new
    for w in range(WALLS):
        out[w] = f[w]


def from_spectrum(spectrum, tables, plain, w):
    cos, sin = plain[0], plain[1]
    both = product(split(spectrum[w]), pair(tables, *BACK), ((1,), (0,)))
    value, turned = both[:, :128], both[:, 128:]
    stacked = jnp.concatenate([value * cos + turned * sin, turned * cos - value * sin], 0)
    return product(pair(tables, *LAST), split(stacked), ((1,), (0,)))


def kernel(
    x_hbm, rate_ref, yf_hbm, tables_hbm, out_ref, x_ref, yf, tables, plain,
    sent, middle, lines, spectrum, damped, damping, rates, numbers,
    returned, middle_back, waves, load_sem, send_sem, recv_sem, rate_sem,
):
    wall, row = lax.axis_index("wall"), lax.axis_index("row")
    low, column = row // COLUMN, row % COLUMN
    plane = wall * 4 + low
    device = wall * 64 + row
    x, z, y, core = plane // 8, plane % 8, column // 2, column % 2

    loads = [
        (x_hbm.at[0], x_ref.at[0]), (yf_hbm, yf), (x_hbm.at[1], x_ref.at[1]), (tables_hbm, tables),
    ]
    loads = [pltpu.make_async_copy(*refs, load_sem.at[k]) for k, refs in enumerate(loads)]
    for load in loads[:3]:
        load.start()

    def column_id(c):
        return wall, low * COLUMN + c

    def plane_id(p):
        return p // 4, lax.rem(p, 4) * COLUMN + column

    def column_peer(h, i):
        half = (y // 4 + 1 - h) % 2
        return (half * 4 + (y + i // 2) % 4) * 2 + (core + i) % 2

    far_x = [(x // 2 + 1) % 2 * 2 + (x + q) % 2 for q in range(2)]

    def far_peer(q, i):
        return far_x[q] * 8 + (z + i) % 8

    def near_peer(i):
        return (x // 2 * 2 + (x + i // 8) % 2) * 8 + (z + i) % 8

    def farthest(t):
        return (4 + (t + 1) // 2 * (1 - 2 * (t % 2))) % 8

    barrier = pltpu.get_barrier_semaphore()

    def greet(to):
        pl.semaphore_signal(barrier, inc=1, device_id=to, device_id_type=MESH)

    for q in range(2):
        for i in (4, 3, 5, 2, 6, 1, 7, 0):
            greet(plane_id(far_peer(q, i)))
    for i in (12, 11, 13, 4, 10, 14, 3, 5, 9, 15, 2, 6, 8, 1, 7):
        greet(plane_id(near_peer(i)))
    for i in range(8):
        greet(column_id(column_peer(0, i)))
    for i in range(7, 0, -1):
        greet(column_id(column_peer(1, i)))

    loads[3].start()

    half_x = [pl.ds(pl.multiple_of((x // 2 + 1 - h) % 2 * 16, 16), 16) for h in range(2)]
    quarter_x = [pl.ds(pl.multiple_of(far_x[q] * 8, 8), 8) for q in range(2)]
    half_y = [pl.ds(pl.multiple_of((y // 4 + 1 - h) % 2 * 8, 8), 8) for h in range(2)]
    done = []

    def remote(src, dst, k, to):
        pltpu.make_async_remote_copy(
            src_ref=src, dst_ref=dst, send_sem=send_sem.at[k], recv_sem=recv_sem.at[k],
            device_id=to, device_id_type=MESH,
        ).start()

    def await_block(src, dst, sem, rows, columns):
        part = (pl.ds(0, rows), pl.ds(0, columns))
        return pltpu.make_async_copy(src.at[part], dst.at[part], sem).wait

    def to_column(src, dst, k, xs, h):
        if h:
            pltpu.make_async_copy(src.at[xs, column], dst.at[xs, column], recv_sem.at[k]).start()

        @pl.loop(0, 8 - h)
        def _(t):
            c = column_peer(h, 7 - t if h else t)
            remote(src.at[xs, c], dst.at[xs, column], k, column_id(c))

    def expect(src, dst, k, rows, columns, out_rows, out_columns):
        done.append(await_block(src, dst, send_sem.at[k], out_rows, out_columns))
        return await_block(src, dst, recv_sem.at[k], rows, columns)

    def far_first(src, mid, k, q):
        xs = quarter_x[q]
        pltpu.make_async_copy(src.at[xs, column], mid.at[xs, column], recv_sem.at[k + q]).start()

        def send(t, other):
            c = (y + farthest(t)) % 8 * 2 + (core + other) % 2
            remote(src.at[xs, c], mid.at[xs, column], k + q, column_id(c))

        @pl.loop(0, 7)
        def _(t):
            send(t, 0)
            send(t, 1)

        send(7, 1)
        return expect(src, mid, k + q, 8, 16, 8, 15)

    def far_second(mid, dst, k, q):
        @pl.loop(0, 8)
        def _(i):
            p = far_peer(q, farthest(i))
            remote(mid.at[p], dst.at[plane], k + 2, plane_id(p))

        return expect(mid, dst, k + 2, 16, 16, 16, 16) if q else None

    def near_first(src, mid, k, q):
        ys = half_y[q]
        pltpu.make_async_copy(
            src.at[plane, ys], mid.at[plane, ys], recv_sem.at[k + 3 + q]
        ).start()

        def send(i):
            p = near_peer(i)
            remote(src.at[p, ys], mid.at[plane, ys], k + 3 + q, plane_id(p))

        @pl.loop(0, 7)
        def _(t):
            send(8 + farthest(t))
            send(farthest(t))

        send(8)

        return expect(src, mid, k + 3 + q, 16, 8, 15, 8)

    def near_second(mid, dst, k, q):
        to_column(mid, dst, k + 5, half_x[1], q)
        return expect(mid, dst, k + 5, 16, 16, 16, 15) if q else None

    zone = lax.broadcasted_iota(jnp.int32, (2, 128), 1) // 32
    value = jnp.broadcast_to(rate_ref[:, 0:1], (2, 128))
    for j in range(1, 4):
        value = jnp.where(zone == j, rate_ref[:, j : j + 1], value)
    numbers[wall] = value
    for s in range(2):
        if s == 0:
            loads[1].wait()
        loads[2 * s].wait()
        to_waves(x_ref[s].reshape(64, N), yf, sent, s)
    pl.semaphore_wait(barrier, PLANE + COLUMN - 2)

    both = (0, 1)
    first_steps = []
    for s in both:
        for q in both:
            near = near_first(sent.at[s], middle.at[s], 6 * s, q)
            first_steps.append(far_first(sent.at[s], middle.at[s], 6 * s, q))
            first_steps.append(near)

    @pl.loop(1, WALLS)
    def _(i):
        pltpu.make_async_remote_copy(
            src_ref=numbers.at[wall], dst_ref=numbers.at[wall],
            send_sem=rate_sem.at[0], recv_sem=rate_sem.at[1],
            device_id=(lax.rem(wall + i, WALLS), row), device_id_type=MESH,
        ).start()

    def second_steps(waits, mid, dst, k):
        for q in both:
            waits[2 * q + 1]()
            near = near_second(mid, dst, k, q)
            waits[2 * q]()
            far = far_second(mid, dst, k, q)
        return far, near

    arrived = [
        second_steps(first_steps[4 * s : 4 * s + 4], middle.at[s], lines.at[s], 6 * s)
        for s in both
    ]

    group = pl.ds(0, WALLS - 1)
    pltpu.make_async_copy(numbers.at[group], numbers.at[group], rate_sem.at[1]).wait()
    for w in range(WALLS):
        for s in both:
            rates[w, s] = jnp.broadcast_to(numbers[w, s : s + 1], (8, 128))
    loads[3].wait()
    for j in range(2):
        terms = [tables[(j, *turn_place(i))].astype(jnp.float32) for i in range(3)]
        plain[j] = terms[0] + (terms[1] + terms[2])
    group_of, m = device // 128, device % 128
    wave = jnp.where(group_of < 3, 8 * m + group_of + 1, 8 * lax.rem(m, 64) + 4 * (m // 64))
    wave = jnp.where(wave > N // 2, wave - N, wave)
    other = jnp.where(device == SPECIAL, N // 2, wave)
    scale = 2.0 * math.pi / N
    scaled, scaled_other = scale * wave.astype(jnp.float32), scale * other.astype(jnp.float32)
    lane = lax.broadcasted_iota(jnp.int32, (64, 128), 1)
    square = jnp.where(lane // 16 % 2 == 0, scaled * scaled, scaled_other * scaled_other)
    wave_x = lax.broadcasted_iota(jnp.int32, (64, 128), 0) + 64 * (lane % 16)
    wave_x = scale * jnp.where(wave_x > N // 2, wave_x - N, wave_x).astype(jnp.float32)
    square = square + wave_x * wave_x
    for s in both:
        set_damping(rates, square, damping, s)

    slabs = [[(x // 2 + 1 - h) % 2 * 4 + j for j in range(4)] for h in both]

    def back_to_lines(s, h):
        for w in slabs[h]:
            lines_back = from_spectrum(damped, tables, plain, w)
            returned[s, pl.ds(4 * w, 4)] = lines_back.reshape(4, 16, 128)

    first_steps = []
    for s in both:
        for h in (1, 0):
            arrived[s][h]()
            for w in slabs[h]:
                to_spectrum(lines, tables, plain, spectrum, s, w)
        diffuse(spectrum, rates, damping, damped, s)
        for h, send in enumerate((far_first, near_first)):
            back_to_lines(s, h)
            for q in both:
                first_steps.append(send(returned.at[s], middle_back.at[s], 12 + 6 * s, q))
    for s in both:
        far0, far1, near0, near1 = first_steps[4 * s : 4 * s + 4]
        waits = far0, near0, far1, near1
        arrived[s] = second_steps(waits, middle_back.at[s], waves.at[s], 12 + 6 * s)
    for s in both:
        for wait in arrived[s]:
            wait()
        from_waves(waves, tables, out_ref, s)
    pltpu.make_async_copy(numbers.at[group], numbers.at[group], rate_sem.at[0]).wait()
    for wait in done:
        wait()


def per_device(thermal_scalars, conductive_number):
    arrays = [jnp.asarray(table) for table in packed_tables()]
    block = pltpu.VMEM((2, PLANE, COLUMN, 128), jnp.float32)
    cube = pltpu.VMEM((2, WALLS, 64, 128), jnp.float32)
    far = pl.BlockSpec(memory_space=pltpu.HBM)
    loaded = [pltpu.VMEM(v.shape, v.dtype) for v in (thermal_scalars, *arrays)]
    result = pl.pallas_call(
        kernel,
        out_shape=jax.ShapeDtypeStruct(thermal_scalars.shape, jnp.float32),
        in_specs=[far, pl.BlockSpec(memory_space=pltpu.VMEM), far, far],
        out_specs=pl.BlockSpec(memory_space=pltpu.VMEM),
        scratch_shapes=[
            *loaded, pltpu.VMEM((2, 64, 128), jnp.float32),
            block, block, block, cube, pltpu.VMEM((WALLS, 64, 128), jnp.float32), cube,
            pltpu.VMEM((WALLS, 2, 8, 128), jnp.float32), pltpu.VMEM((WALLS, 2, 128), jnp.float32),
            block, block, block,
            pltpu.SemaphoreType.DMA((4,)), pltpu.SemaphoreType.DMA((24,)),
            pltpu.SemaphoreType.DMA((24,)), pltpu.SemaphoreType.DMA((2,)),
        ],
        compiler_params=pltpu.CompilerParams(
            collective_id=0, has_side_effects=True, vmem_limit_bytes=VMEM_LIMIT
        ),
    )(thermal_scalars, conductive_number, *arrays)
    return result * (2.0 / (N * N))


def solution(mesh):
    return jax.shard_map(
        per_device,
        mesh=mesh,
        in_specs=(P(None, "wall", "row", None), P(None, "wall")),
        out_specs=P(None, "wall", "row", None),
        check_vma=False,
    )
```

```python
import functools
import math

import jax
import jax.numpy as jnp
import numpy as np
from jax import lax
from jax.experimental import pallas as pl
from jax.experimental.pallas import tpu as pltpu
from jax.sharding import PartitionSpec as P

STEPS = 3
MESH = pl.DeviceIdType.MESH
N = 1024
COLUMN = 16
PLANE = 32
WALLS = 8
SPECIAL = 384
HALF = math.sqrt(0.5)
VMEM_LIMIT = 54400 << 10


def halves(table):
    table = np.asarray(table, np.float32)
    high = table.astype(jnp.bfloat16)
    low = (table - high.astype(np.float32)).astype(jnp.bfloat16)
    return np.stack([high, low])


def y_tables():
    b = np.arange(128)[None, :]
    m = np.arange(128)[:, None]
    forward, inverse = [], []
    for n in (1, 2, 3):
        angle = 2 * np.pi * ((b * (8 * m + n)) % N) / N
        c, s = np.cos(angle), np.sin(angle)
        forward.append(np.concatenate([c, s], 1))
        inverse.append(np.block([[c, s], [-s, c]]))
    m = m[:64]
    zero = 2 * np.pi * ((b * 8 * m) % N) / N
    four = 2 * np.pi * ((b * (8 * m + 4)) % N) / N
    c0, s0, c4, s4 = np.cos(zero), np.sin(zero), np.cos(four), np.sin(four)
    flip = np.where(b % 2 == 0, 1.0, -1.0)
    s0[:1] = -flip
    forward.append(np.block([[c0, s0], [c4, s4]]))
    c0[:1] *= 0.5
    s0[:1] *= 0.5
    none = np.zeros_like(c0)
    inverse.append(np.block([[c0, none], [none, c4], [-s0, none], [none, -s4]]))
    return np.stack(forward), np.stack(inverse)


def x_tables():
    n = np.arange(64)
    angle = 2 * np.pi * ((n[:, None] * n[None, :]) % 64) / 64
    c, s = np.cos(angle), np.sin(angle)
    first = np.concatenate([c, s], 0)
    last = np.concatenate([c, s], 1)
    i = np.arange(16)
    small = 2 * np.pi * ((i[:, None] * i[None, :]) % 16) / 16
    c, s = np.cos(small), np.sin(small)
    into = np.zeros((2, 2, 4, 16, 4, 2, 16))
    back = np.zeros((4, 2, 16, 2, 2, 4, 16))
    for part in range(2):
        for z in range(4):
            into[0, part, z, :, z, part] = c + s
            into[1, part, z, :, z, part] = c - s
            back[z, part, :, 0, part, z] = c + s
            back[z, part, :, 1, part, z] = c - s
    into, back = into.reshape(256, 128), back.reshape(128, 256)
    lane = np.arange(128)
    turn = 2 * np.pi * (n[:, None] * (lane % 16)[None, :]) / N
    return first, last, into, back, np.cos(turn), np.sin(turn)


def packed_tables():
    forward, inverse = y_tables()
    first, last, into, back, cos, sin = x_tables()
    packed = np.zeros((2, 1664, 256), jnp.bfloat16)
    packed[:, :1024] = halves(inverse.reshape(1024, 256))
    for table, place in ((back, BACK), (into, INTO), (last, LAST), (first, FIRST)):
        packed[(slice(None), *place)] = halves(table)
    for j, table in enumerate((cos, sin)):
        rest = table.astype(np.float32)
        for i in range(3):
            term = rest.astype(jnp.bfloat16)
            packed[(j, *turn_place(i))] = term
            rest = rest - term.astype(np.float32)
    return halves(forward), packed


def turn_place(i):
    return slice(1408 + 64 * i, 1472 + 64 * i), slice(0, 128)


BACK = slice(1024, 1152), slice(0, 256)
INTO = slice(1152, 1408), slice(0, 128)
LAST = slice(1152, 1216), slice(128, 256)
FIRST = slice(1216, 1344), slice(128, 192)


def split(value):
    high = value.astype(jnp.bfloat16)
    return high, (value - high.astype(jnp.float32)).astype(jnp.bfloat16)


def product(left, right, dims):
    dot = functools.partial(
        lax.dot_general, dimension_numbers=(dims, ((), ())), preferred_element_type=jnp.float32
    )
    return dot(left[0], right[0]) + (dot(left[0], right[1]) + dot(left[1], right[0]))


def pair(ref, *index):
    return ref[(0, *index)], ref[(1, *index)]


def to_waves(field, table, out, s):
    f = [field[:, 128 * a : 128 * a + 128] for a in range(8)]
    s04, d04, s26, d26 = f[0] + f[4], f[0] - f[4], f[2] + f[6], f[2] - f[6]
    s15, d15, s37, d37 = f[1] + f[5], f[1] - f[5], f[3] + f[7], f[3] - f[7]
    even, odd = s04 + s26, s15 + s37
    less, more = HALF * (d15 - d37), HALF * (d15 + d37)
    none = jnp.zeros_like(even)
    parts = [
        (d04 + less, -d26 - more),
        (s04 - s26, s37 - s15),
        (d04 - less, d26 - more),
    ]
    for j, (re, im) in enumerate(parts):
        both = jnp.concatenate(
            [jnp.concatenate([re, im], 1), jnp.concatenate([im, -re], 1)], 0
        )
        waves = product(pair(table, j), split(both), ((1,), (1,)))
        out[s, 8 * j : 8 * j + 8] = waves.reshape(8, 16, 128)
    for j, re in enumerate((even + odd, even - odd)):
        both = jnp.concatenate(
            [jnp.concatenate([re, none], 1), jnp.concatenate([none, -re], 1)], 0
        )
        rows = slice(64 * j, 64 * j + 64)
        waves = product(pair(table, 3, rows), split(both), ((1,), (1,)))
        out[s, 24 + 4 * j : 28 + 4 * j] = waves.reshape(4, 16, 128)


def from_waves(waves, table, out, s):
    u = []
    for j in range(4):
        lines = waves[s, 8 * j : 8 * j + 8].reshape(128, 128).T
        both = jnp.concatenate([lines[:64], lines[64:]], 1)
        u.append(product(split(both), pair(table, slice(256 * j, 256 * j + 256)), ((1,), (0,))))
    (re1, im1), (re2, im2), (re3, im3), (z0, z4) = [(v[:, :128], v[:, 128:]) for v in u]
    plus, minus = z0 + z4, z0 - z4
    even = [plus + re2, minus - im2, plus - re2, minus + im2]
    odd = [
        re1 + re3,
        HALF * ((re1 - im1) - (re3 + im3)),
        im3 - im1,
        HALF * ((re3 - im3) - (re1 + im1)),
    ]
    for a in range(4):
        out[s, :, :, 128 * a : 128 * a + 128] = (even[a] + odd[a]).reshape(4, 16, 128)
        out[s, :, :, 128 * a + 512 : 128 * a + 640] = (even[a] - odd[a]).reshape(4, 16, 128)


def to_spectrum(lines, tables, plain, out, s, w):
    cos, sin = plain[0], plain[1]
    block = lines[s, pl.ds(4 * w, 4)].reshape(64, 128)
    both = product(pair(tables, *FIRST), split(block), ((1,), (0,)))
    c, t = both[:64], both[64:]
    turned = jnp.concatenate([c * cos - t * sin, c * sin + t * cos], 1)
    out[s, w] = product(split(turned), pair(tables, *INTO), ((1,), (0,)))


def set_damping(rates, square, out, s):
    for w in range(WALLS):
        rate = jnp.concatenate([rates[w, s]] * 8, 0)
        out[s, w] = jnp.exp(-rate * square)


def diffuse(spectrum, rates, damping, out, s):
    lane = lax.broadcasted_iota(jnp.int32, (64, 128), 1)
    low, high = lane < 32, lane >= 96
    none = jnp.zeros((64, 128), jnp.float32)
    f = [spectrum[s, w] for w in range(WALLS)]
    for step in range(STEPS):
        new = []
        for w in range(WALLS):
            above = f[w + 1] if w + 1 < WALLS else none
            below = f[w - 1] if w else none
            up = pltpu.roll(jnp.where(low, above, f[w]), 96, 1)
            down = pltpu.roll(jnp.where(high, below, f[w]), 32, 1)
            rate = jnp.concatenate([rates[w, s]] * 8, 0)
            new.append(damping[s, w] * (f[w] + rate * (up + down - 2.0 * f[w])))
        f = new
    for w in range(WALLS):
        out[w] = f[w]


def from_spectrum(spectrum, tables, plain, w):
    cos, sin = plain[0], plain[1]
    both = product(split(spectrum[w]), pair(tables, *BACK), ((1,), (0,)))
    value, turned = both[:, :128], both[:, 128:]
    stacked = jnp.concatenate([value * cos + turned * sin, turned * cos - value * sin], 0)
    return product(pair(tables, *LAST), split(stacked), ((1,), (0,)))


def kernel(
    x_hbm, rate_ref, yf_hbm, tables_hbm, out_ref, x_ref, yf, tables, plain,
    sent, middle, lines, spectrum, damped, damping, rates, numbers,
    returned, middle_back, waves, load_sem, send_sem, recv_sem, rate_sem,
):
    wall, row = lax.axis_index("wall"), lax.axis_index("row")
    low, column = row // COLUMN, row % COLUMN
    plane = wall * 4 + low
    device = wall * 64 + row
    x, z, y, core = plane // 8, plane % 8, column // 2, column % 2

    loads = [
        (x_hbm.at[0], x_ref.at[0]), (yf_hbm, yf), (x_hbm.at[1], x_ref.at[1]), (tables_hbm, tables),
    ]
    loads = [pltpu.make_async_copy(*refs, load_sem.at[k]) for k, refs in enumerate(loads)]
    for load in loads[:3]:
        load.start()

    def column_id(c):
        return wall, low * COLUMN + c

    def plane_id(p):
        return p // 4, lax.rem(p, 4) * COLUMN + column

    def column_peer(h, i):
        half = (y // 4 + 1 - h) % 2
        return (half * 4 + (y + i // 2) % 4) * 2 + (core + i) % 2

    far_x = [(x // 2 + 1) % 2 * 2 + (x + q) % 2 for q in range(2)]

    def far_peer(q, i):
        return far_x[q] * 8 + (z + i) % 8

    def near_peer(i):
        return (x // 2 * 2 + (x + i // 8) % 2) * 8 + (z + i) % 8

    def farthest(t):
        return (4 + (t + 1) // 2 * (1 - 2 * (t % 2))) % 8

    barrier = pltpu.get_barrier_semaphore()

    def greet(to):
        pl.semaphore_signal(barrier, inc=1, device_id=to, device_id_type=MESH)

    for q in range(2):
        for i in (4, 3, 5, 2, 6, 1, 7, 0):
            greet(plane_id(far_peer(q, i)))
    for i in (12, 11, 13, 4, 10, 14, 3, 5, 9, 15, 2, 6, 8, 1, 7):
        greet(plane_id(near_peer(i)))
    for i in range(8):
        greet(column_id(column_peer(0, i)))
    for i in range(7, 0, -1):
        greet(column_id(column_peer(1, i)))

    loads[3].start()

    half_x = [pl.ds(pl.multiple_of((x // 2 + 1 - h) % 2 * 16, 16), 16) for h in range(2)]
    quarter_x = [pl.ds(pl.multiple_of(far_x[q] * 8, 8), 8) for q in range(2)]
    half_y = [pl.ds(pl.multiple_of((y // 4 + 1 - h) % 2 * 8, 8), 8) for h in range(2)]
    done = []

    def remote(src, dst, k, to):
        pltpu.make_async_remote_copy(
            src_ref=src, dst_ref=dst, send_sem=send_sem.at[k], recv_sem=recv_sem.at[k],
            device_id=to, device_id_type=MESH,
        ).start()

    def await_block(src, dst, sem, rows, columns):
        part = (pl.ds(0, rows), pl.ds(0, columns))
        return pltpu.make_async_copy(src.at[part], dst.at[part], sem).wait

    def to_column(src, dst, k, xs, h):
        if h:
            pltpu.make_async_copy(src.at[xs, column], dst.at[xs, column], recv_sem.at[k]).start()

        @pl.loop(0, 8 - h)
        def _(t):
            c = column_peer(h, 7 - t if h else t)
            remote(src.at[xs, c], dst.at[xs, column], k, column_id(c))

    def expect(src, dst, k, rows, columns, out_rows, out_columns):
        done.append(await_block(src, dst, send_sem.at[k], out_rows, out_columns))
        return await_block(src, dst, recv_sem.at[k], rows, columns)

    def far_first(src, mid, k, q):
        xs = quarter_x[q]
        pltpu.make_async_copy(src.at[xs, column], mid.at[xs, column], recv_sem.at[k + q]).start()

        def send(t, other):
            c = (y + farthest(t)) % 8 * 2 + (core + other) % 2
            remote(src.at[xs, c], mid.at[xs, column], k + q, column_id(c))

        @pl.loop(0, 7)
        def _(t):
            send(t, 0)
            send(t, 1)

        send(7, 1)
        return expect(src, mid, k + q, 8, 16, 8, 15)

    def far_second(mid, dst, k, q):
        @pl.loop(0, 8)
        def _(i):
            p = far_peer(q, farthest(i))
            remote(mid.at[p], dst.at[plane], k + 2, plane_id(p))

        return expect(mid, dst, k + 2, 16, 16, 16, 16) if q else None

    def near_first(src, mid, k, q):
        ys = half_y[q]
        pltpu.make_async_copy(
            src.at[plane, ys], mid.at[plane, ys], recv_sem.at[k + 3 + q]
        ).start()

        def send(i):
            p = near_peer(i)
            remote(src.at[p, ys], mid.at[plane, ys], k + 3 + q, plane_id(p))

        @pl.loop(0, 7)
        def _(t):
            send(8 + farthest(t))
            send(farthest(t))

        send(8)

        return expect(src, mid, k + 3 + q, 16, 8, 15, 8)

    def both_first(src, mid, k, q):
        xs, ys = quarter_x[q], half_y[q]
        local = [
            (src.at[plane, ys], mid.at[plane, ys], k + 3 + q),
            (src.at[xs, column], mid.at[xs, column], k + q),
        ]
        for here, there, sem in local:
            pltpu.make_async_copy(here, there, recv_sem.at[sem]).start()

        def near(i):
            p = near_peer(i)
            remote(src.at[p, ys], mid.at[plane, ys], k + 3 + q, plane_id(p))

        def far(t, other):
            c = (y + farthest(t)) % 8 * 2 + (core + other) % 2
            remote(src.at[xs, c], mid.at[xs, column], k + q, column_id(c))

        @pl.loop(0, 7)
        def _(t):
            near(8 + farthest(t))
            far(t, 0)
            near(farthest(t))
            far(t, 1)

        near(8)
        far(7, 1)
        return [
            expect(src, mid, k + q, 8, 16, 8, 15),
            expect(src, mid, k + 3 + q, 16, 8, 15, 8),
        ]

    def near_second(mid, dst, k, q):
        to_column(mid, dst, k + 5, half_x[1], q)
        return expect(mid, dst, k + 5, 16, 16, 16, 15) if q else None

    zone = lax.broadcasted_iota(jnp.int32, (2, 128), 1) // 32
    value = jnp.broadcast_to(rate_ref[:, 0:1], (2, 128))
    for j in range(1, 4):
        value = jnp.where(zone == j, rate_ref[:, j : j + 1], value)
    numbers[wall] = value
    for s in range(2):
        if s == 0:
            loads[1].wait()
        loads[2 * s].wait()
        to_waves(x_ref[s].reshape(64, N), yf, sent, s)
    pl.semaphore_wait(barrier, PLANE + COLUMN - 2)

    both = (0, 1)
    first_steps = []
    for s in both:
        for q in both:
            first_steps += both_first(sent.at[s], middle.at[s], 6 * s, q)

    @pl.loop(1, WALLS)
    def _(i):
        pltpu.make_async_remote_copy(
            src_ref=numbers.at[wall], dst_ref=numbers.at[wall],
            send_sem=rate_sem.at[0], recv_sem=rate_sem.at[1],
            device_id=(lax.rem(wall + i, WALLS), row), device_id_type=MESH,
        ).start()

    def second_steps(waits, mid, dst, k):
        for q in both:
            waits[2 * q + 1]()
            near = near_second(mid, dst, k, q)
            waits[2 * q]()
            far = far_second(mid, dst, k, q)
        return far, near

    arrived = [
        second_steps(first_steps[4 * s : 4 * s + 4], middle.at[s], lines.at[s], 6 * s)
        for s in both
    ]

    group = pl.ds(0, WALLS - 1)
    pltpu.make_async_copy(numbers.at[group], numbers.at[group], rate_sem.at[1]).wait()
    for w in range(WALLS):
        for s in both:
            rates[w, s] = jnp.broadcast_to(numbers[w, s : s + 1], (8, 128))
    loads[3].wait()
    for j in range(2):
        terms = [tables[(j, *turn_place(i))].astype(jnp.float32) for i in range(3)]
        plain[j] = terms[0] + (terms[1] + terms[2])
    group_of, m = device // 128, device % 128
    wave = jnp.where(group_of < 3, 8 * m + group_of + 1, 8 * lax.rem(m, 64) + 4 * (m // 64))
    wave = jnp.where(wave > N // 2, wave - N, wave)
    other = jnp.where(device == SPECIAL, N // 2, wave)
    scale = 2.0 * math.pi / N
    scaled, scaled_other = scale * wave.astype(jnp.float32), scale * other.astype(jnp.float32)
    lane = lax.broadcasted_iota(jnp.int32, (64, 128), 1)
    square = jnp.where(lane // 16 % 2 == 0, scaled * scaled, scaled_other * scaled_other)
    wave_x = lax.broadcasted_iota(jnp.int32, (64, 128), 0) + 64 * (lane % 16)
    wave_x = scale * jnp.where(wave_x > N // 2, wave_x - N, wave_x).astype(jnp.float32)
    square = square + wave_x * wave_x
    for s in both:
        set_damping(rates, square, damping, s)

    slabs = [[(x // 2 + 1 - h) % 2 * 4 + j for j in range(4)] for h in both]

    def back_to_lines(s, h):
        for w in slabs[h]:
            lines_back = from_spectrum(damped, tables, plain, w)
            returned[s, pl.ds(4 * w, 4)] = lines_back.reshape(4, 16, 128)

    first_steps = []
    for s in both:
        for h in (1, 0):
            arrived[s][h]()
            for w in slabs[h]:
                to_spectrum(lines, tables, plain, spectrum, s, w)
        diffuse(spectrum, rates, damping, damped, s)
        for h, send in enumerate((far_first, near_first)):
            back_to_lines(s, h)
            for q in both:
                first_steps.append(send(returned.at[s], middle_back.at[s], 12 + 6 * s, q))
    for s in both:
        far0, far1, near0, near1 = first_steps[4 * s : 4 * s + 4]
        waits = far0, near0, far1, near1
        arrived[s] = second_steps(waits, middle_back.at[s], waves.at[s], 12 + 6 * s)
    for s in both:
        for wait in arrived[s]:
            wait()
        from_waves(waves, tables, out_ref, s)
    pltpu.make_async_copy(numbers.at[group], numbers.at[group], rate_sem.at[0]).wait()
    for wait in done:
        wait()


def per_device(thermal_scalars, conductive_number):
    arrays = [jnp.asarray(table) for table in packed_tables()]
    block = pltpu.VMEM((2, PLANE, COLUMN, 128), jnp.float32)
    cube = pltpu.VMEM((2, WALLS, 64, 128), jnp.float32)
    far = pl.BlockSpec(memory_space=pltpu.HBM)
    loaded = [pltpu.VMEM(v.shape, v.dtype) for v in (thermal_scalars, *arrays)]
    result = pl.pallas_call(
        kernel,
        out_shape=jax.ShapeDtypeStruct(thermal_scalars.shape, jnp.float32),
        in_specs=[far, pl.BlockSpec(memory_space=pltpu.VMEM), far, far],
        out_specs=pl.BlockSpec(memory_space=pltpu.VMEM),
        scratch_shapes=[
            *loaded, pltpu.VMEM((2, 64, 128), jnp.float32),
            block, block, block, cube, pltpu.VMEM((WALLS, 64, 128), jnp.float32), cube,
            pltpu.VMEM((WALLS, 2, 8, 128), jnp.float32), pltpu.VMEM((WALLS, 2, 128), jnp.float32),
            block, block, block,
            pltpu.SemaphoreType.DMA((4,)), pltpu.SemaphoreType.DMA((24,)),
            pltpu.SemaphoreType.DMA((24,)), pltpu.SemaphoreType.DMA((2,)),
        ],
        compiler_params=pltpu.CompilerParams(
            collective_id=0, has_side_effects=True, vmem_limit_bytes=VMEM_LIMIT
        ),
    )(thermal_scalars, conductive_number, *arrays)
    return result * (2.0 / (N * N))


def solution(mesh):
    return jax.shard_map(
        per_device,
        mesh=mesh,
        in_specs=(P(None, "wall", "row", None), P(None, "wall")),
        out_specs=P(None, "wall", "row", None),
        check_vma=False,
    )
```
